32 devices in a mesh: dp: 8 (over y, x, core), tensor: 4 (over z).
Axes of the slice: x: 2, y: 2, z: 4, core: 2. Of those that a mesh axis runs over, the one named last changes fastest.
Arguments:
- hidden_in: bfloat16 [8192, 768], P('dp'), may hold values from -40 to 40
- segment_ids: int32 [8, 1024], P('dp'), may hold values from 0 to 5, never falling along the last dimension, each value on 1 to 512 neighbouring positions
- norm_weight: float32 [768], replicated, may hold values from 0.5 to 1.5
- w_z: bfloat16 [768, 1536], P(None, 'tensor'), may hold values from -0.5 to 0.5
- w_x: bfloat16 [768, 1536], P(None, 'tensor'), may hold values from -0.21875 to 0.21875
- w_bc: bfloat16 [768, 256], replicated, may hold values from -0.21875 to 0.21875
- w_dt: bfloat16 [768, 24], P(None, 'tensor'), may hold values from -0.21875 to 0.21875
- conv_x: float32 [4, 1536], P(None, 'tensor'), may hold values from -3 to 3
- conv_x_bias: float32 [1536], P('tensor'), may hold values from -3 to 3
- conv_bc: float32 [4, 256], replicated, may hold values from -3 to 3
- conv_bc_bias: float32 [256], replicated, may hold values from -3 to 3
- dt_bias: float32 [24], P('tensor'), may hold values from -4 to -1
- a_log: float32 [24], P('tensor'), may hold values from -7 to 0.5
- d_skip: float32 [24], P('tensor'), may hold values from 0.5 to 2
- gate_norm_weight: float32 [1536], P('tensor'), may hold values from 0.5 to 1.5
- w_out: bfloat16 [1536, 768], P('tensor'), may hold values from -0.15625 to 0.15625
- out_grad: bfloat16 [8192, 768], P('dp'), may hold values from -6 to 6
Outputs:
- block_out: bfloat16 [8192, 768], P('dp')
- in_grad: float32 [8192, 768], P('dp')
- grad_norm_weight: float32 [768], replicated
- grad_w_z: float32 [768, 1536], P(None, 'tensor')
- grad_w_x: float32 [768, 1536], P(None, 'tensor')
- grad_w_bc: float32 [768, 256], replicated
- grad_w_dt: float32 [768, 24], P(None, 'tensor')
- grad_conv_x: float32 [4, 1536], P(None, 'tensor')
- grad_conv_x_bias: float32 [1536], P('tensor')
- grad_conv_bc: float32 [4, 256], replicated
- grad_conv_bc_bias: float32 [256], replicated
- grad_dt_bias: float32 [24], P('tensor')
- grad_a_log: float32 [24], P('tensor')
- grad_d_skip: float32 [24], P('tensor')
- grad_gate_norm_weight: float32 [1536], P('tensor')
- grad_w_out: float32 [1536, 768], P('tensor')
The draws below stay inside these ranges and needn't reach their ends.
Inputs may be any that keep to these rules, and one draw needn't show every extreme that they name: `segment_ids`: segment numbers never fall along a sequence; sequence s holds the tokens s * 1024 to (s + 1) * 1024 - 1 of hidden_in and out_grad.
All inputs are finite; a program needn't handle non-finite values.
Results may differ from the reference program's by a relative error of at most 0.02.
Values may be sent and summed in bfloat16 or wider, within the bound.
No kernel may reach another device: no remote copies, remote signals or barrier semaphores. Data moves between devices by JAX's collectives and lax.ppermute only.
A program may use at most 128 MiB of HBM per device.

```python
import math
import jax
import jax.numpy as jnp
import numpy as np
from jax import lax

D = 768
H = 24
P_SIZE = 64
N = 128
KC = 4
SEQ_LEN = 1024
SEG_COUNT = 6
DI = 1536
SEG_MOST = 512
SEQS = 8
TOKENS = 8192
N_TENSOR = 4


def draw_hidden_in(key, part):
    key_rows = jax.random.fold_in(key, 11)
    key_cols = jax.random.fold_in(key, 12)
    key_base = jax.random.fold_in(key, 13)
    row_scale = jnp.exp(jax.random.uniform(key_rows, (TOKENS, 1), jnp.float32, math.log(0.3), math.log(3.0)))
    col_scale = jnp.exp(jax.random.uniform(key_cols, (1, D), jnp.float32, math.log(0.4), math.log(2.5)))
    base = jax.random.normal(key_base, (TOKENS, D), jnp.float32)
    values = base * row_scale * col_scale
    return jnp.clip(values, -40.0, 40.0).astype(jnp.bfloat16)


def draw_w_z(key, part):
    key_base = jax.random.fold_in(key, 21)
    ramp = jnp.arange(DI).astype(jnp.float32) / (DI - 1)
    scale = 0.6 * jnp.exp(ramp * math.log(3.0))
    base = jax.random.normal(key_base, (D, DI), jnp.float32)
    values = base * scale[None, :] / math.sqrt(D)
    return jnp.clip(values, -0.5, 0.5).astype(jnp.bfloat16)


def shard_levels(stream_key, shape, shards, low, largest):
    loudness = 1.0
    for dim, blocks in shards:
        steps = jax.random.uniform(jax.random.fold_in(jax.random.fold_in(stream_key, 6), dim), (blocks,), jnp.float32, low / len(shards), largest / len(shards))
        loudness = loudness * jnp.repeat(jnp.exp(steps), shape[dim] // blocks).reshape((-1,) + (1,) * (len(shape) - 1 - dim))
    return loudness


def profile(amount, total, most, lean):
    weights = [(1 << 20) // math.isqrt(standing ** lean) + 1 for standing in range(2, amount + 1)]
    surplus, given = total - most - (amount - 1), [1] * (amount - 1)
    while surplus > 0:
        free = [i for i in range(amount - 1) if given[i] < most]
        whole, left = sum([weights[i] for i in free]), surplus
        for i in free:
            addition = min(most - given[i], max(1, left * weights[i] // whole), surplus)
            given[i] = given[i] + addition
            surplus = surplus - addition
    return np.array([most] + given)


def uneven_parts(rng, count, total, most, skew):
    if count == 2:
        one = jax.random.randint(rng, (), max(1, total - most), min(most, total - 1) + 1)
        return jnp.stack([one, total - one])
    lengths = jnp.asarray(profile(count, total, most, skew), jnp.int32)
    twos = (count - 1) // 2
    donor, receiver = lengths[1:1 + 2 * twos:2], lengths[2:2 + 2 * twos:2]
    room = jnp.minimum(donor - 1, most - receiver)
    shifted = jax.random.randint(jax.random.fold_in(rng, 1), (twos,), 0, 1 << 20) % (room + 1)
    lengths = lengths.at[1:1 + 2 * twos:2].set(donor - shifted).at[2:2 + 2 * twos:2].set(receiver + shifted)
    return lengths[jax.random.permutation(jax.random.fold_in(rng, 2), count)]


def bell_draw(own_key, extent, scale, reach, cuts=(), held_as=jnp.bfloat16):
    entries = jax.random.normal(own_key, extent, jnp.float32) * scale
    if len(cuts) > 0:
        entries = shard_levels(own_key, extent, cuts, -0.22, 0.18) * entries
    return jnp.clip(entries, min=-reach, max=reach).astype(held_as)


def setup_inputs(seed: int = 0) -> dict:
    arg_keys = jax.random.split(jax.random.key(seed), 18)
    return {
        "hidden_in": draw_hidden_in(jax.random.fold_in(arg_keys[17], 71), 0),
        "segment_ids": jax.vmap(lambda own: jnp.searchsorted(jnp.cumsum(uneven_parts(own, SEG_COUNT, SEQ_LEN, SEG_MOST, 1)), jnp.arange(SEQ_LEN), side="right"))(jax.random.split(arg_keys[1], SEQS)).reshape((SEQS, SEQ_LEN)).astype(jnp.int32),
        "norm_weight": jnp.clip(1.0 + 0.1 * jax.random.normal(arg_keys[2], (D,), jnp.float32), 0.5, 1.5),
        "w_z": draw_w_z(jax.random.fold_in(arg_keys[17], 71), 0),
        "w_x": bell_draw(arg_keys[4], (D, DI), D ** -0.5, 0.21875, ((1, 4),)),
        "w_bc": bell_draw(arg_keys[5], (D, 2 * N), D ** -0.5, 0.21875),
        "w_dt": bell_draw(arg_keys[6], (D, H), D ** -0.5, 0.21875, ((1, 4),)),
        "conv_x": bell_draw(arg_keys[7], (KC, DI), 0.5, 3.0, ((1, 4),), jnp.float32),
        "conv_x_bias": bell_draw(arg_keys[8], (DI,), 0.3, 3.0, ((0, 4),), jnp.float32),
        "conv_bc": bell_draw(arg_keys[9], (KC, 2 * N), 0.5, 3.0, (), jnp.float32),
        "conv_bc_bias": bell_draw(arg_keys[10], (2 * N,), 0.3, 3.0, (), jnp.float32),
        "dt_bias": jnp.clip(-4.0 + 3.0 * jax.random.uniform(arg_keys[11], (H,), jnp.float32) ** shard_levels(arg_keys[11], (H,), ((0, 4),), -0.2, 0.2), -4.0, -1.0),
        "a_log": jnp.clip(-7.0 + 7.5 * jax.random.uniform(arg_keys[12], (H,), jnp.float32) ** shard_levels(arg_keys[12], (H,), ((0, 4),), -0.2, 0.2), -7.0, 0.5),
        "d_skip": jnp.clip(0.5 + 1.5 * jax.random.uniform(arg_keys[13], (H,), jnp.float32) ** shard_levels(arg_keys[13], (H,), ((0, 4),), -0.2, 0.2), 0.5, 2.0),
        "gate_norm_weight": jnp.clip(1.0 + 0.1 * jax.random.normal(arg_keys[14], (DI,), jnp.float32), 0.5, 1.5),
        "w_out": bell_draw(arg_keys[15], (DI, D), DI ** -0.5, 0.15625, ((0, 4),)),
        "out_grad": bell_draw(arg_keys[16], (TOKENS, D), 1.0, 6.0, ((0, 8),)),
    }


HIGH = lax.Precision.HIGHEST
EPS = 1e-05

def silu_grad(values):
    sig = jax.nn.sigmoid(values)
    return sig * (1.0 + values * (1.0 - sig))

def lag_rows(values, lag_size):
    if lag_size == 0:
        return values
    return jnp.pad(values[:values.shape[0] - lag_size], ((lag_size, 0), (0, 0)))

def same_rows(segments, lag_size):
    if lag_size == 0:
        return jnp.ones((segments.shape[0], 1), jnp.float32)
    earlier = jnp.pad(segments[:segments.shape[0] - lag_size], (lag_size, 0), constant_values=-1)
    return (earlier == segments).astype(jnp.float32)[:, None]

def conv_forward(values, taps, bias, segments):
    total = jnp.zeros_like(values) + bias
    for tap_index in range(taps.shape[0]):
        lag_size = taps.shape[0] - 1 - tap_index
        total = total + taps[tap_index] * lag_rows(values, lag_size) * same_rows(segments, lag_size)
    return total

def conv_backward(values, taps, pre_act, grad_post, segments):
    grad_pre = grad_post * silu_grad(pre_act)
    grad_bias = lax.optimization_barrier(jnp.sum(grad_pre, 0))
    grad_in = jnp.zeros_like(values)
    tap_grads = []
    for tap_index in range(taps.shape[0]):
        lag_size = taps.shape[0] - 1 - tap_index
        keep = same_rows(segments, lag_size)
        tap_grads.append(lax.optimization_barrier(jnp.sum(grad_pre * lag_rows(values, lag_size) * keep, 0)))
        masked = grad_pre * keep * taps[tap_index]
        if lag_size > 0:
            masked = jnp.pad(masked[lag_size:], ((0, lag_size), (0, 0)))
        grad_in = grad_in + masked
    return (grad_in, jnp.stack(tap_grads), grad_bias)

def causal_mask(segments):
    positions = jnp.arange(segments.shape[0])
    return (positions[:, None] >= positions[None, :]) & (segments[:, None] == segments[None, :])

def head_forward(gram_mat, same_mask, cum_decay, scaled_x):
    gap = jnp.where(same_mask, cum_decay[:, None] - cum_decay[None, :], 0.0)
    weights = jnp.where(same_mask, gram_mat * jnp.exp(gap), 0.0)
    return jnp.dot(weights, scaled_x, precision=HIGH)

def head_backward(gram_mat, same_mask, cum_decay, scaled_x, grad_out):
    gap = jnp.where(same_mask, cum_decay[:, None] - cum_decay[None, :], 0.0)
    decay = jnp.where(same_mask, jnp.exp(gap), 0.0)
    weights = gram_mat * decay
    grad_x = jnp.dot(weights.T, grad_out, precision=HIGH)
    grad_wt = jnp.dot(grad_out, scaled_x.T, precision=HIGH)
    flow = grad_wt * weights
    grad_cum = lax.optimization_barrier(jnp.sum(flow, 1)) - lax.optimization_barrier(jnp.sum(flow, 0))
    return (grad_x, grad_wt * decay, grad_cum)

def sequence_pass(params, inputs_bf, segments, grad_bf):
    norm_weight, w_z, w_x, w_bc, w_dt, conv_x, conv_x_bias, conv_bc, conv_bc_bias, dt_bias, a_log, d_skip, gate_norm_weight, w_out = params
    length = segments.shape[0]
    group = DI // N_TENSOR
    hgroup = H // N_TENSOR
    inputs = inputs_bf.astype(jnp.float32)
    rstd = lax.rsqrt(lax.optimization_barrier(jnp.mean(inputs * inputs, axis=1, keepdims=True)) + EPS)
    normed = (inputs * rstd * norm_weight).astype(jnp.bfloat16)
    gate_pre = jnp.dot(normed, w_z, preferred_element_type=jnp.float32)
    x_raw = jnp.dot(normed, w_x, preferred_element_type=jnp.float32)
    bc_raw = jnp.dot(normed, w_bc, preferred_element_type=jnp.float32)
    dt_raw = jnp.dot(normed, w_dt, preferred_element_type=jnp.float32)
    x_pre = conv_forward(x_raw, conv_x, conv_x_bias, segments)
    x_conv = jax.nn.silu(x_pre)
    bc_pre = conv_forward(bc_raw, conv_bc, conv_bc_bias, segments)
    bc_conv = jax.nn.silu(bc_pre)
    b_mat = bc_conv[:, :N]
    c_mat = bc_conv[:, N:]
    dt_val = dt_raw + dt_bias
    step_size = jax.nn.softplus(dt_val)
    rate = -jnp.exp(a_log)
    decay = step_size * rate
    cum_decay = jnp.cumsum(decay, axis=0)
    gram_mat = jnp.dot(c_mat, b_mat.T, precision=HIGH)
    same_mask = causal_mask(segments)
    x_heads = x_conv.reshape(length, H, P_SIZE)
    scaled = step_size[:, :, None] * x_heads
    ssd_heads = lax.map(lambda pair: head_forward(gram_mat, same_mask, pair[0], pair[1]), (cum_decay.T, scaled.transpose(1, 0, 2)))
    ssd_heads = ssd_heads.transpose(1, 0, 2) + d_skip[:, None] * x_heads
    ssd_out = ssd_heads.reshape(length, DI)
    gate_act = jax.nn.silu(gate_pre)
    gated = ssd_out * gate_act
    gate_rstd = lax.rsqrt(lax.optimization_barrier(jnp.sum(gated * gated, axis=1, keepdims=True)) / DI + EPS)
    normed_out = (gated * gate_rstd * gate_norm_weight).astype(jnp.bfloat16)
    partials = jnp.einsum('tkc,kcd->tkd', normed_out.reshape(length, N_TENSOR, group).astype(jnp.float32), w_out.reshape(N_TENSOR, group, D).astype(jnp.float32), precision=HIGH)
    partials = lax.optimization_barrier(partials.astype(jnp.bfloat16))
    mixed = lax.optimization_barrier(jnp.sum(partials.astype(jnp.float32), axis=1))
    block_out = (inputs + mixed).astype(jnp.bfloat16)
    out_cot = grad_bf.astype(jnp.float32)
    grad_w_out = jnp.dot(normed_out.T, grad_bf, preferred_element_type=jnp.float32)
    grad_norm_out = jnp.dot(grad_bf, w_out.T, preferred_element_type=jnp.float32)
    grad_gate_norm_weight = lax.optimization_barrier(jnp.sum(grad_norm_out * gated * gate_rstd, 0))
    gscaled = grad_norm_out * gate_norm_weight
    gate_stat = lax.optimization_barrier(jnp.sum(gscaled * gated, axis=1, keepdims=True))
    grad_gated = gate_rstd * gscaled - gated * gate_rstd ** 3 * gate_stat / DI
    grad_ssd = grad_gated * gate_act
    grad_gate = grad_gated * ssd_out * silu_grad(gate_pre)
    grad_heads = grad_ssd.reshape(length, H, P_SIZE)
    grad_d_skip = lax.optimization_barrier(jnp.sum(grad_heads * x_heads, axis=(0, 2)))

    def head_step(carry, quad):
        grad_x, grad_gram, grad_cum = head_backward(gram_mat, same_mask, quad[1], quad[2], quad[3])
        return (carry.at[quad[0] // hgroup].add(grad_gram), (grad_x, grad_cum))
    head_ids = jnp.arange(H).astype(jnp.int32)
    grad_gram_groups, (grad_scaled, grad_cum) = lax.scan(head_step, jnp.zeros((N_TENSOR, length, length), jnp.float32), (head_ids, cum_decay.T, scaled.transpose(1, 0, 2), grad_heads.transpose(1, 0, 2)))
    grad_scaled = grad_scaled.transpose(1, 0, 2)
    grad_cum = grad_cum.T
    grad_decay = jnp.flip(jnp.cumsum(jnp.flip(grad_cum, 0), axis=0), 0)
    grad_xs = grad_heads * d_skip[:, None] + grad_scaled * step_size[:, :, None]
    grad_step = lax.optimization_barrier(jnp.sum(grad_scaled * x_heads, axis=2)) + grad_decay * rate
    grad_a_log = lax.optimization_barrier(jnp.sum(grad_decay * decay, 0))
    grad_dtv = grad_step * jax.nn.sigmoid(dt_val)
    grad_dt_bias = lax.optimization_barrier(jnp.sum(grad_dtv, 0))
    grad_c_groups = jnp.einsum('kts,sn->ktn', grad_gram_groups, b_mat, precision=HIGH)
    grad_b_groups = jnp.einsum('kts,tn->ksn', grad_gram_groups, c_mat, precision=HIGH)
    grad_bc_groups = jnp.concatenate([grad_b_groups, grad_c_groups], axis=2)
    raw_groups, taps_groups, bias_groups = jax.vmap(conv_backward, in_axes=(None, None, None, 0, None))(bc_raw, conv_bc, bc_pre, grad_bc_groups, segments)
    grad_bc_raw = lax.optimization_barrier(jnp.sum(raw_groups, 0))
    grad_conv_bc = lax.optimization_barrier(jnp.sum(taps_groups, 0))
    grad_conv_bc_bias = lax.optimization_barrier(jnp.sum(bias_groups, 0))
    grad_x_raw, grad_conv_x, grad_conv_x_bias = conv_backward(x_raw, conv_x, x_pre, grad_xs.reshape(length, DI), segments)
    grad_gate_b = grad_gate.astype(jnp.bfloat16)
    grad_x_b = grad_x_raw.astype(jnp.bfloat16)
    grad_dt_b = grad_dtv.astype(jnp.bfloat16)
    grad_w_z = jnp.dot(normed.T, grad_gate_b, preferred_element_type=jnp.float32)
    grad_w_x = jnp.dot(normed.T, grad_x_b, preferred_element_type=jnp.float32)
    grad_w_dt = jnp.dot(normed.T, grad_dt_b, preferred_element_type=jnp.float32)
    grad_w_bc = jnp.dot(normed.astype(jnp.float32).T, grad_bc_raw, precision=HIGH)
    part_sum = jnp.einsum('tkc,dkc->tkd', grad_gate_b.reshape(length, N_TENSOR, group).astype(jnp.float32), w_z.reshape(D, N_TENSOR, group).astype(jnp.float32), precision=HIGH)
    part_sum = part_sum + jnp.einsum('tkc,dkc->tkd', grad_x_b.reshape(length, N_TENSOR, group).astype(jnp.float32), w_x.reshape(D, N_TENSOR, group).astype(jnp.float32), precision=HIGH)
    part_sum = part_sum + jnp.einsum('tkc,dkc->tkd', grad_dt_b.reshape(length, N_TENSOR, hgroup).astype(jnp.float32), w_dt.reshape(D, N_TENSOR, hgroup).astype(jnp.float32), precision=HIGH)
    part_sum = part_sum + jnp.einsum('ktc,dc->tkd', raw_groups, w_bc.astype(jnp.float32), precision=HIGH)
    part_sum = lax.optimization_barrier(part_sum.astype(jnp.bfloat16))
    grad_normed = lax.optimization_barrier(jnp.sum(part_sum.astype(jnp.float32), axis=1))
    grad_norm_weight = lax.optimization_barrier(jnp.sum(grad_normed * inputs * rstd, 0))
    gnorm = grad_normed * norm_weight
    in_grad = out_cot + rstd * gnorm - inputs * rstd ** 3 * lax.optimization_barrier(jnp.mean(gnorm * inputs, axis=1, keepdims=True))
    grads = (grad_norm_weight, grad_w_z, grad_w_x, grad_w_bc, grad_w_dt, grad_conv_x, grad_conv_x_bias, grad_conv_bc, grad_conv_bc_bias, grad_dt_bias, grad_a_log, grad_d_skip, grad_gate_norm_weight, grad_w_out)
    return (block_out, in_grad, grads)

def reference(hidden_in, segment_ids, norm_weight, w_z, w_x, w_bc, w_dt, conv_x, conv_x_bias, conv_bc, conv_bc_bias, dt_bias, a_log, d_skip, gate_norm_weight, w_out, out_grad):
    params = (norm_weight, w_z, w_x, w_bc, w_dt, conv_x, conv_x_bias, conv_bc, conv_bc_bias, dt_bias, a_log, d_skip, gate_norm_weight, w_out)
    start = tuple((jnp.zeros(item.shape, jnp.float32) for item in params))

    def seq_step(carry, slices):
        block_out, in_grad, grads = sequence_pass(params, slices[0], slices[1], slices[2])
        return (tuple((left + right for left, right in zip(carry, grads))), (block_out, in_grad))
    grads, (block_out, in_grad) = lax.scan(seq_step, start, (hidden_in.reshape(SEQS, SEQ_LEN, D), segment_ids, out_grad.reshape(SEQS, SEQ_LEN, D)))
    return (block_out.reshape(TOKENS, D), in_grad.reshape(TOKENS, D), grads[0], grads[1], grads[2], grads[3], grads[4], grads[5], grads[6], grads[7], grads[8], grads[9], grads[10], grads[11], grads[12], grads[13])
```

```python
import functools

import jax
import jax.numpy as jnp
from jax import lax
from jax.experimental import pallas as pl
from jax.experimental.pallas import tpu as pltpu
from jax.sharding import PartitionSpec as P

EPS = 1e-05
HIGH = lax.Precision.HIGHEST
F32 = jnp.float32
BF = jnp.bfloat16
NEG = -1e30
CHUNK = 256
HP = 8
TAIL = 8


def dot(a, b, prec=None):
    return lax.dot_general(a, b, (((1,), (0,)), ((), ())), precision=prec, preferred_element_type=F32)


def dot_nt(a, b, prec=None):
    return lax.dot_general(a, b, (((1,), (1,)), ((), ())), precision=prec, preferred_element_type=F32)


def dot_tn(a, b, prec=None):
    return lax.dot_general(a, b, (((0,), (0,)), ((), ())), precision=prec, preferred_element_type=F32)


def sigmoid(v):
    return 1.0 / (1.0 + jnp.exp(-v))


def softplus(v):
    return jnp.maximum(v, 0.0) + jnp.log1p(jnp.exp(-jnp.abs(v)))


def lane_tiles(width):
    return [(j, min(128, width - j)) for j in range(0, width, 128)]


def expand(cols, base, width, psize):
    rows = cols.shape[0]
    out = []
    for j, w in lane_tiles(width):
        first = base + j // psize
        tile = jnp.broadcast_to(cols[:, first : first + 1], (rows, w))
        lane = lax.broadcasted_iota(jnp.int32, (rows, w), 1)
        for extra in range(1, w // psize):
            tile = jnp.where(
                lane >= extra * psize,
                jnp.broadcast_to(cols[:, first + extra : first + extra + 1], (rows, w)),
                tile,
            )
        out.append(tile)
    return jnp.concatenate(out, axis=1) if len(out) > 1 else out[0]


def head_rows(width, psize):
    row = lax.broadcasted_iota(jnp.int32, (HP, width), 0)
    lane = lax.broadcasted_iota(jnp.int32, (HP, width), 1)
    return ((lane >= row * psize) & (lane < (row + 1) * psize)).astype(F32)


def chunk_mask(segcol, segrow):
    size = segcol.shape[0]
    row = lax.broadcasted_iota(jnp.int32, (size, size), 0)
    col = lax.broadcasted_iota(jnp.int32, (size, size), 1)
    return (row >= col) & (segcol == segrow)


def decay_rows(dtv, alog, rows):
    size = dtv.shape[1]
    step = softplus(dtv)
    rate = -jnp.exp(alog)
    decay = step * rate
    row = lax.broadcasted_iota(jnp.int32, (size, size), 0)
    col = lax.broadcasted_iota(jnp.int32, (size, size), 1)
    cum = dot(decay, (row <= col).astype(F32), HIGH)
    end = cum[:, size - 1 : size]
    ein = jnp.exp(cum) * rows[1:2]
    eout = jnp.exp(end - cum) * rows[2:3]
    return step, rate, decay, cum, ein, eout


def columns_of(*parts):
    stack = jnp.concatenate(parts, axis=0)
    pad = 128 - stack.shape[0]
    if pad:
        stack = jnp.concatenate([stack, jnp.zeros((pad, stack.shape[1]), F32)], axis=0)
    return stack.T


def fwd_kernel(
    psize, hid, og, cols, rows, nw, wz, wx, wbc, wdt, cx, cxb, cbc, cbcb, dtb, alog, dskip, gnw, wout,
    normed_o, gate_o, xraw_o, xpre_o, bcraw_o, bcpre_o, dtv_o, y_o, gno_o, st_o, q_o, stats_o,
    xbuf, bcbuf, state,
):
    size = hid.shape[0]
    width = wz.shape[1]
    heads = width // psize
    nst = wbc.shape[1] // 2

    @pl.when(pl.program_id(0) == 0)
    def _():
        xbuf[0:TAIL, :] = jnp.zeros((TAIL, width), F32)
        bcbuf[0:TAIL, :] = jnp.zeros((TAIL, 2 * nst), F32)
        state[...] = jnp.zeros_like(state)

    inputs = hid[...].astype(F32)
    rstd = lax.rsqrt(jnp.mean(inputs * inputs, axis=1, keepdims=True) + EPS)
    normed = (inputs * rstd * nw[...]).astype(BF)
    normed_o[...] = normed
    gate = dot(normed, wz[...])
    gate_o[...] = gate
    xraw = dot(normed, wx[...])
    bcraw = dot(normed, wbc[...])
    xraw_o[...] = xraw
    bcraw_o[...] = bcraw
    dtv = dot_nt(wdt[...], normed) + dtb[...]
    dtv_o[...] = dtv

    c = cols[...]
    xbuf[TAIL:, :] = xraw
    bcbuf[TAIL:, :] = bcraw
    xpre = cxb[...] + cx[3:4, :] * xraw
    bcpre = cbcb[...] + cbc[3:4, :] * bcraw
    for lag in (1, 2, 3):
        keep = c[:, lag - 1 : lag]
        xpre += cx[3 - lag : 4 - lag, :] * (xbuf[TAIL - lag : TAIL - lag + size, :] * keep)
        bcpre += cbc[3 - lag : 4 - lag, :] * (bcbuf[TAIL - lag : TAIL - lag + size, :] * keep)
    xbuf[0:TAIL, :] = xbuf[size : size + TAIL, :]
    bcbuf[0:TAIL, :] = bcbuf[size : size + TAIL, :]
    xpre_o[...] = xpre
    bcpre_o[...] = bcpre
    xs = xpre * sigmoid(xpre)
    bc = (bcpre * sigmoid(bcpre)).astype(BF)
    b_b = bc[:, :nst]
    c_b = bc[:, nst:]

    step, rate, decay, cum, ein, eout = decay_rows(dtv, alog[...], rows[...])
    tcol = columns_of(step, cum, ein, eout)
    scaled = expand(tcol, 0, width, psize) * xs
    scaled_b = scaled.astype(BF)
    bias = jnp.where(chunk_mask(c[:, 8:9], rows[0:1, :]), 0.0, NEG)
    gram = dot_nt(c_b, b_b)
    state_b = state[...].astype(BF)
    st_o[0] = state_b
    carry = ein[:, size - 1 : size]
    cross = dot(c_b, state_b)
    ein_e = expand(tcol, 2 * HP, width, psize)
    ytiles = []
    for j, w in lane_tiles(width):
        lane = lax.broadcasted_iota(jnp.int32, (size, w), 1)
        tile = None
        for e in range(w // psize):
            h = j // psize + e
            dec = jnp.exp(tcol[:, HP + h : HP + h + 1] - cum[h : h + 1, :] + bias)
            got = dot((gram * dec).astype(BF), scaled_b[:, j : j + w])
            tile = got if tile is None else jnp.where(lane >= e * psize, got, tile)
        ytiles.append(tile)
    y = jnp.concatenate(ytiles, axis=1) if len(ytiles) > 1 else ytiles[0]
    y = y + ein_e * cross
    sent = (expand(tcol, 3 * HP, width, psize) * scaled).astype(BF)
    carry_e = expand(jnp.broadcast_to(tcol[size - 8 : size, :], (8, 128)), 2 * HP, width, psize)[7:8, :]
    state[...] = carry_e * state[...] + dot_tn(b_b, sent)
    y = y + dskip[...] * xs
    y_o[...] = y
    gated = y * (gate * sigmoid(gate))
    gno = dot_nt(og[...], wout[...])
    gno_o[...] = gno
    weighted = gated * gnw[...]
    ones = jnp.ones((HP, width), F32)
    sq = dot_nt(ones, gated * gated, HIGH)
    gs = dot_nt(ones, gno * weighted, HIGH)
    pick = lax.broadcasted_iota(jnp.int32, (HP, size), 0)
    stats_o[...] = jnp.where(pick == 0, sq, jnp.where(pick == 1, gs, 0.0))
    q_o[...] = dot(weighted.astype(BF), wout[...]).astype(BF)


def bwd_kernel(
    psize, di, hid, og, cols, rows, normed_r, gate_r, xraw_r, xpre_r, bcraw_r, bcpre_r, dtv_r, y_r, gno_r, st_r, stats_r,
    wz, wx, wbc, wdt, cx, cbc, alog, dskip, gnw,
    part_o, gwz_o, gwx_o, gwbc_o, gwo_o, gwdt_o, gcx_o, gcbc_o, ggn_o, gnw_o, gh_o,
    xbuf, bcbuf, ds, awz, awx, awbc, awo, gcar,
):
    size = hid.shape[0]
    width = wz.shape[1]
    nst = wbc.shape[1] // 2
    step_id = pl.program_id(0)

    @pl.when(step_id == 0)
    def _():
        xbuf[size:, :] = jnp.zeros((TAIL, width), F32)
        bcbuf[size:, :] = jnp.zeros((TAIL, 2 * nst), F32)
        for ref in (ds, awz, awx, awbc, awo, gcar, gwdt_o, gcx_o, gcbc_o, ggn_o, gnw_o, gh_o):
            ref[...] = jnp.zeros_like(ref)

    inputs = hid[...].astype(F32)
    in_rstd = lax.rsqrt(jnp.mean(inputs * inputs, axis=1, keepdims=True) + EPS)
    normed = normed_r[...]
    gate = gate_r[...]
    y = y_r[...]
    c = cols[...]
    stats = stats_r[...]
    r_rstd = lax.rsqrt(stats[0:1] / di + EPS)
    r_beta = r_rstd * r_rstd * r_rstd * stats[1:2] / di
    step, rate, decay, cum, ein, eout = decay_rows(dtv_r[...], alog[...], rows[...])
    pickr = lax.broadcasted_iota(jnp.int32, (HP, size), 0)
    tcol = columns_of(step, cum, ein, eout, jnp.where(pickr == 0, r_rstd, r_beta))
    rstd = tcol[:, 4 * HP : 4 * HP + 1]
    beta = tcol[:, 4 * HP + 1 : 4 * HP + 2]

    sig = sigmoid(gate)
    act = gate * sig
    gated = y * act
    gno = gno_r[...]
    grs = gated * rstd
    ggn_o[0:1, :] += jnp.sum(gno * grs, axis=0, keepdims=True)
    normed_out = (grs * gnw[...]).astype(BF)
    awo[...] += dot_tn(normed_out, og[...])
    ggated = rstd * (gno * gnw[...]) - gated * beta
    dy = ggated * act
    ggate_b = (ggated * y * (sig * (1.0 + gate * (1.0 - sig)))).astype(BF)

    xpre = xpre_r[...]
    xsig = sigmoid(xpre)
    xs = xpre * xsig
    step_e = expand(tcol, 0, width, psize)
    scaled = step_e * xs
    scaled_b = scaled.astype(BF)
    dy_b = dy.astype(BF)
    bcpre = bcpre_r[...]
    bcsig = sigmoid(bcpre)
    bc = (bcpre * bcsig).astype(BF)
    b_b = bc[:, :nst]
    c_b = bc[:, nst:]
    mask = chunk_mask(c[:, 8:9], rows[0:1, :])
    bias = jnp.where(mask, 0.0, NEG)
    gram = dot_nt(c_b, b_b)
    dgram = jnp.zeros((size, size), F32)
    gtiles = []
    for j, w in lane_tiles(width):
        lane = lax.broadcasted_iota(jnp.int32, (size, w), 1)
        tile = None
        for e in range(w // psize):
            h = j // psize + e
            dec = jnp.exp(tcol[:, HP + h : HP + h + 1] - cum[h : h + 1, :] + bias)
            weights = (gram * dec).astype(BF)
            got = dot_tn(weights, dy_b[:, j : j + w])
            tile = got if tile is None else jnp.where(lane >= e * psize, got, tile)
            mine = (lane >= e * psize) & (lane < (e + 1) * psize)
            left = jnp.where(mine, dy[:, j : j + w], 0.0).astype(BF)
            dgram += dot_nt(left, scaled_b[:, j : j + w]) * dec
        gtiles.append(tile)
    gsc = jnp.concatenate(gtiles, axis=1) if len(gtiles) > 1 else gtiles[0]
    ds_b = ds[...].astype(BF)
    st_b = st_r[0]
    ein_e = expand(tcol, 2 * HP, width, psize)
    eout_e = expand(tcol, 3 * HP, width, psize)
    gsc += eout_e * dot(b_b, ds_b)
    sent = (eout_e * scaled).astype(BF)
    seen = (ein_e * dy).astype(BF)
    dgram_b = dgram.astype(BF)
    gb = dot_tn(dgram_b, c_b) + dot_nt(sent, ds_b)
    gc = dot(dgram_b, b_b) + dot_nt(seen, st_b)
    carry_e = ein_e[size - 1 : size, :]
    ds[...] = carry_e * ds[...] + dot_tn(c_b, seen)

    hr = head_rows(width, psize)
    y_ns = y - dskip[...] * xs
    gcum = dot_nt(hr, dy_b.astype(F32) * y_ns - scaled_b.astype(F32) * gsc, HIGH)
    gdecay = dot(gcum, mask.astype(F32), HIGH) + gcar[:, 0:1] * rows[3:4, :]
    gcar[:, 0:1] = gdecay[:, 0:1]
    gstep = dot_nt(hr, gsc * xs, HIGH) + gdecay * rate
    gdtv = gstep * sigmoid(dtv_r[...])
    gds = dot_nt(hr, dy * xs, HIGH)
    gh_o[:, 0:1] += jnp.sum(gdecay * decay, axis=1, keepdims=True)
    gh_o[:, 1:2] += jnp.sum(gdtv, axis=1, keepdims=True)
    gh_o[:, 2:3] += jnp.sum(gds, axis=1, keepdims=True)
    gwdt_o[...] += dot(gdtv.astype(BF), normed)
    gdt_col = columns_of(gdtv)[:, 0:HP].astype(BF)

    gxp = (dy * dskip[...] + gsc * step_e) * (xsig * (1.0 + xpre * (1.0 - xsig)))
    xraw = xraw_r[...]
    bcraw = bcraw_r[...]
    gbp = jnp.concatenate([gb, gc], axis=1) * (bcsig * (1.0 + bcpre * (1.0 - bcsig)))
    xbuf[0:size, :] = gxp
    bcbuf[0:size, :] = gbp
    gx = cx[3:4, :] * gxp
    gbc = cbc[3:4, :] * gbp
    gcx_o[3:4, :] += jnp.sum(gxp * xraw, axis=0, keepdims=True)
    gcbc_o[3:4, :] += jnp.sum(gbp * bcraw, axis=0, keepdims=True)
    gcx_o[4:5, :] += jnp.sum(gxp, axis=0, keepdims=True)
    gcbc_o[4:5, :] += jnp.sum(gbp, axis=0, keepdims=True)
    for lag in (1, 2, 3):
        keep = c[:, 2 + lag : 3 + lag]
        moved = xbuf[lag : lag + size, :] * keep
        gx += cx[3 - lag : 4 - lag, :] * moved
        gcx_o[3 - lag : 4 - lag, :] += jnp.sum(moved * xraw, axis=0, keepdims=True)
        moved = bcbuf[lag : lag + size, :] * keep
        gbc += cbc[3 - lag : 4 - lag, :] * moved
        gcbc_o[3 - lag : 4 - lag, :] += jnp.sum(moved * bcraw, axis=0, keepdims=True)
    xbuf[size:, :] = gxp[0:TAIL, :]
    bcbuf[size:, :] = gbp[0:TAIL, :]
    gx_b = gx.astype(BF)
    gbc_b = gbc.astype(BF)
    nt = normed.T
    awz[...] += dot(nt, ggate_b)
    awx[...] += dot(nt, gx_b)
    awbc[...] += dot(nt, gbc_b)
    part = dot_nt(ggate_b, wz[...]) + dot_nt(gx_b, wx[...]) + dot_nt(gbc_b, wbc[...]) + dot(gdt_col, wdt[...])
    part_o[...] = part.astype(BF)
    gnw_o[0:1, :] += jnp.sum(part * (inputs * in_rstd), axis=0, keepdims=True)

    @pl.when(step_id == pl.num_programs(0) - 1)
    def _():
        gwz_o[...] = awz[...].astype(BF)
        gwx_o[...] = awx[...].astype(BF)
        gwbc_o[...] = awbc[...].astype(BF)
        gwo_o[...] = awo[...].astype(BF)


def final_kernel(hid, og, mixed_r, grad_r, rstd_r, nw, block_o, ingrad_o):
    inputs = hid[...].astype(F32)
    rstd = lax.rsqrt(jnp.mean(inputs * inputs, axis=1, keepdims=True) + EPS)
    block_o[...] = (inputs + rstd_r[...] * mixed_r[...].astype(F32)).astype(BF)
    gn = grad_r[...].astype(F32) * nw[...]
    mean = jnp.mean(gn * inputs, axis=1, keepdims=True)
    ingrad_o[...] = og[...].astype(F32) + rstd * gn - inputs * (rstd * rstd * rstd * mean)


def local(
    hidden_in, segment_ids, norm_weight, w_z, w_x, w_bc, w_dt, conv_x, conv_x_bias, conv_bc, conv_bc_bias,
    dt_bias, a_log, d_skip, gate_norm_weight, w_out, out_grad, n_tensor,
):
    seg = segment_ids[0]
    total = seg.shape[0]
    dim = hidden_in.shape[1]
    heads = dt_bias.shape[0]
    width = w_z.shape[1]
    psize = width // heads
    nst = w_bc.shape[1] // 2
    di = width * n_tensor
    size = min(CHUNK, total)
    nc = total // size

    def lagged(n):
        if n > 0:
            other = jnp.concatenate([jnp.full((n,), -1, seg.dtype), seg[:-n]])
        else:
            other = jnp.concatenate([seg[-n:], jnp.full((-n,), -1, seg.dtype)])
        return (other == seg).astype(F32)

    seg2 = seg.reshape(nc, size)
    none = jnp.full((1,), -1, seg.dtype)
    before = jnp.concatenate([none, seg2[:-1, -1]])[:, None]
    after = jnp.concatenate([seg2[1:, 0], none])[:, None]
    inm = (seg2 == before).astype(F32).reshape(total)
    outm = (seg2 == seg2[:, -1:]).astype(F32).reshape(total)
    nxm = (seg2 == after).astype(F32).reshape(total)
    segf = seg.astype(F32)
    cols = jnp.stack([lagged(1), lagged(2), lagged(3), lagged(-1), lagged(-2), lagged(-3), inm, outm, segf], axis=1)
    rows = jnp.stack([segf, inm, outm, nxm] + [segf] * 4, axis=0)
    wdt = jnp.pad(w_dt.T, ((0, HP - heads), (0, 0)))
    dtb = jnp.pad(dt_bias, (0, HP - heads))[:, None]
    alog = jnp.pad(a_log, (0, HP - heads))[:, None]
    dsk = jnp.repeat(d_skip, psize)[None]
    gnw = gate_norm_weight[None]
    nw = norm_weight[None]

    def tok(w):
        return pl.BlockSpec((size, w), lambda i: (i, 0))

    def tokr(w):
        return pl.BlockSpec((size, w), lambda i: (nc - 1 - i, 0))

    def rowf(h):
        return pl.BlockSpec((h, size), lambda i: (0, i))

    def rowb(h):
        return pl.BlockSpec((h, size), lambda i: (0, nc - 1 - i))

    def whole(a):
        return pl.BlockSpec(a.shape, lambda i: (0,) * len(a.shape))

    def out(shape, dt):
        return jax.ShapeDtypeStruct(shape, dt)

    fixed = (nw, w_z, w_x, w_bc, wdt, conv_x, conv_x_bias[None], conv_bc, conv_bc_bias[None], dtb, alog, dsk, gnw, w_out)
    saved = pl.pallas_call(
        functools.partial(fwd_kernel, psize),
        grid=(nc,),
        in_specs=[tok(dim), tok(dim), tok(9), rowf(HP)] + [whole(a) for a in fixed],
        out_specs=[
            tok(dim), tok(width), tok(width), tok(width), tok(2 * nst), tok(2 * nst), rowf(HP), tok(width), tok(width),
            pl.BlockSpec((1, nst, width), lambda i: (i, 0, 0)), tok(dim), rowf(HP),
        ],
        out_shape=[
            out((total, dim), BF), out((total, width), F32), out((total, width), F32), out((total, width), F32),
            out((total, 2 * nst), F32), out((total, 2 * nst), F32), out((HP, total), F32), out((total, width), F32),
            out((total, width), F32), out((nc, nst, width), BF), out((total, dim), BF), out((HP, total), F32),
        ],
        scratch_shapes=[
            pltpu.VMEM((size + TAIL, width), F32), pltpu.VMEM((size + TAIL, 2 * nst), F32), pltpu.VMEM((nst, width), F32),
        ],
        name="fwd",
    )(hidden_in, out_grad, cols, rows, *fixed)
    normed, gate, xraw, xpre, bcraw, bcpre, dtv, y, gno, states, q, stats = saved
    stats = lax.psum(stats, "tensor")
    mixed = lax.psum(q, "tensor")

    fixed2 = (w_z, w_x, w_bc, wdt, conv_x, conv_bc, alog, dsk, gnw)
    accs = [(dim, width), (dim, width), (dim, 2 * nst), (width, dim)]
    small = [(HP, dim), (HP, width), (HP, 2 * nst), (HP, width), (HP, dim), (HP, 128)]
    res = pl.pallas_call(
        functools.partial(bwd_kernel, psize, di),
        grid=(nc,),
        in_specs=[
            tokr(dim), tokr(dim), tokr(9), rowb(HP), tokr(dim), tokr(width), tokr(width), tokr(width), tokr(2 * nst),
            tokr(2 * nst), rowb(HP), tokr(width), tokr(width),
            pl.BlockSpec((1, nst, width), lambda i: (nc - 1 - i, 0, 0)), rowb(HP),
        ] + [whole(a) for a in fixed2],
        out_specs=[tokr(dim)] + [pl.BlockSpec(s, lambda i: (0, 0)) for s in accs + small],
        out_shape=[out((total, dim), BF)] + [out(s, BF) for s in accs] + [out(s, F32) for s in small],
        scratch_shapes=[
            pltpu.VMEM((size + TAIL, width), F32), pltpu.VMEM((size + TAIL, 2 * nst), F32), pltpu.VMEM((nst, width), F32),
        ] + [pltpu.VMEM(s, F32) for s in accs] + [pltpu.VMEM((HP, 128), F32)],
        name="bwd",
    )(hidden_in, out_grad, cols, rows, normed, gate, xraw, xpre, bcraw, bcpre, dtv, y, gno, states, stats, *fixed2)
    part, gwz, gwx, gwbc, gwo, gwdt, gcx, gcbc, ggn, gnw_p, gh = res
    grad = lax.psum(part, "tensor")
    rstd_col = lax.rsqrt(stats[0] / di + EPS)[:, None]
    block_out, in_grad = pl.pallas_call(
        final_kernel,
        grid=(nc,),
        in_specs=[tok(dim), tok(dim), tok(dim), tok(dim), tok(1), whole(nw)],
        out_specs=[tok(dim), tok(dim)],
        out_shape=[out((total, dim), BF), out((total, dim), F32)],
        name="final",
    )(hidden_in, out_grad, mixed, grad, rstd_col, nw)
    gwz, gwx, gwo, gwdt, gcx, ggn, gh = lax.psum(
        (gwz, gwx, gwo, gwdt.astype(BF), gcx.astype(BF), ggn[0].astype(BF), gh.astype(BF)), "dp"
    )
    gwbc, gcbc, gnw_p = lax.psum((gwbc, gcbc.astype(BF), gnw_p[0].astype(BF)), ("dp", "tensor"))
    return (
        block_out,
        in_grad,
        gnw_p.astype(F32),
        gwz.astype(F32),
        gwx.astype(F32),
        gwbc.astype(F32),
        gwdt[:heads].T.astype(F32),
        gcx[:4].astype(F32),
        gcx[4].astype(F32),
        gcbc[:4].astype(F32),
        gcbc[4].astype(F32),
        gh[:heads, 1].astype(F32),
        gh[:heads, 0].astype(F32),
        gh[:heads, 2].astype(F32),
        ggn.astype(F32),
        gwo.astype(F32),
    )


def solution(mesh):
    t = P(None, "tensor")
    return jax.shard_map(
        functools.partial(local, n_tensor=mesh.shape["tensor"]),
        mesh=mesh,
        in_specs=(
            P("dp", None), P("dp", None), P(), t, t, P(), t, t, P("tensor"), P(), P(),
            P("tensor"), P("tensor"), P("tensor"), P("tensor"), P("tensor", None), P("dp", None),
        ),
        out_specs=(
            P("dp", None), P("dp", None), P(), t, t, P(), t, t, P("tensor"), P(), P(),
            P("tensor"), P("tensor"), P("tensor"), P("tensor"), P("tensor", None),
        ),
        check_vma=False,
    )
```

```python
import functools

import jax
import jax.numpy as jnp
from jax import lax
from jax.experimental import pallas as pl
from jax.experimental.pallas import tpu as pltpu
from jax.sharding import PartitionSpec as P

EPS = 1e-05
HIGH = lax.Precision.HIGHEST
F32 = jnp.float32
BF = jnp.bfloat16
NEG = -1e30
CHUNK = 256
HP = 8
TAIL = 8


def dot(a, b, prec=None):
    return lax.dot_general(a, b, (((1,), (0,)), ((), ())), precision=prec, preferred_element_type=F32)


def dot_nt(a, b, prec=None):
    return lax.dot_general(a, b, (((1,), (1,)), ((), ())), precision=prec, preferred_element_type=F32)


def dot_tn(a, b, prec=None):
    return lax.dot_general(a, b, (((0,), (0,)), ((), ())), precision=prec, preferred_element_type=F32)


def sigmoid(v):
    return 0.5 * jnp.tanh(0.5 * v) + 0.5


def split3(v):
    a = v.astype(BF)
    left = v - a.astype(F32)
    b = left.astype(BF)
    return jnp.concatenate([a.astype(F32), b.astype(F32), left - b.astype(F32)], axis=0).astype(BF)


def rows_dot(v, ones):
    got = dot(split3(v), ones)
    n = v.shape[0]
    return got[0:n] + got[n : 2 * n] + got[2 * n : 3 * n]


def head_sums(v, base, psize):
    width = v.shape[1]
    unit = lax.broadcasted_iota(jnp.int32, (width, 128), 0)
    lane = lax.broadcasted_iota(jnp.int32, (width, 128), 1) - base
    mark = jnp.where((unit >= lane * psize) & (unit < (lane + 1) * psize), 1.0, 0.0).astype(BF)
    big = v.astype(BF)
    return dot(big, mark) + dot((v - big.astype(F32)).astype(BF), mark)


def softplus(v):
    return jnp.maximum(v, 0.0) + jnp.log1p(jnp.exp(-jnp.abs(v)))


def lane_tiles(width):
    return [(j, min(128, width - j)) for j in range(0, width, 128)]


def expand(cols, base, width, psize):
    rows = cols.shape[0]
    out = []
    for j, w in lane_tiles(width):
        first = base + j // psize
        tile = jnp.broadcast_to(cols[:, first : first + 1], (rows, w))
        lane = lax.broadcasted_iota(jnp.int32, (rows, w), 1)
        for extra in range(1, w // psize):
            tile = jnp.where(
                lane >= extra * psize,
                jnp.broadcast_to(cols[:, first + extra : first + extra + 1], (rows, w)),
                tile,
            )
        out.append(tile)
    return jnp.concatenate(out, axis=1) if len(out) > 1 else out[0]


def chunk_mask(segcol, segrow):
    size = segcol.shape[0]
    row = lax.broadcasted_iota(jnp.int32, (size, size), 0)
    col = lax.broadcasted_iota(jnp.int32, (size, size), 1)
    return (row >= col) & (segcol == segrow)


def decay_rows(dtv, alog, inm, outm):
    size = dtv.shape[1]
    step = softplus(dtv)
    rate = -jnp.exp(alog)
    decay = step * rate
    row = lax.broadcasted_iota(jnp.int32, (size, size), 0)
    col = lax.broadcasted_iota(jnp.int32, (size, size), 1)
    cum = rows_dot(decay, jnp.where(row <= col, 1.0, 0.0).astype(BF))
    end = cum[:, size - 1 : size]
    ein = jnp.exp(cum) * inm
    eout = jnp.exp(end - cum) * outm
    return step, rate, decay, cum, ein, eout


def columns_of(*parts):
    stack = jnp.concatenate(parts, axis=0)
    pad = 128 - stack.shape[0]
    if pad:
        stack = jnp.concatenate([stack, jnp.zeros((pad, stack.shape[1]), F32)], axis=0)
    return stack.T


def fill_rows(seg_ref, rows_s, size):
    total = seg_ref.shape[1]
    seg = seg_ref[...].astype(F32)
    wide = jnp.broadcast_to(seg, (8, total))
    lane = lax.broadcasted_iota(jnp.int32, (8, total), 1)
    rows_s[...] = jnp.zeros_like(rows_s)
    rows_s[0:1, :] = seg
    for lag in (1, 2, 3):
        back = (pltpu.roll(wide, lag, 1) == wide) & (lane >= lag)
        rows_s[3 + lag : 4 + lag, :] = jnp.where(back, 1.0, 0.0)[0:1]
        ahead = (pltpu.roll(wide, total - lag, 1) == wide) & (lane < total - lag)
        rows_s[6 + lag : 7 + lag, :] = jnp.where(ahead, 1.0, 0.0)[0:1]
    for start in range(0, total, size):
        end = start + size
        part = seg[:, start:end]
        if start:
            rows_s[1:2, start:end] = jnp.where(part == seg[:, start - 1 : start], 1.0, 0.0)
        rows_s[2:3, start:end] = jnp.where(part == seg[:, end - 1 : end], 1.0, 0.0)
        if end < total:
            rows_s[3:4, start:end] = jnp.where(part == seg[:, end : end + 1], 1.0, 0.0)


def row_of(ref):
    return ref[...].reshape(1, -1)


def fill_params(heads, wdt, dtb, alog, dsk, wd_s, hb):
    wd_s[...] = jnp.zeros_like(wd_s)
    wd_s[0:heads, :] = wdt[...].astype(F32)
    hb[...] = jnp.zeros_like(hb)
    for i, ref in enumerate((dtb, alog, dsk)):
        hb[i : i + 1, 0:heads] = row_of(ref)


def head_params(hb, width, psize):
    rows = hb[...]
    cols = square([rows]).T
    skip = expand(rows, 0, width, psize)[2:3, :]
    return cols[0:HP, 0:1], cols[0:HP, 1:2], skip


def fwd_kernel(
    psize, c0, hid, og, seg, nw, wz, wx, wbc, wdt, cx, cxb, cbc, cbcb, dtb_r, alog_r, dsk_r, gnw, wout, *rest,
):
    if c0:
        xt_r, bt_r, sin_r = rest[:3]
        rest = rest[3:]
    normed_o, gate_o, xraw_o, xpre_o, bcraw_o, bcpre_o, dtv_o, y_o, gno_o, st_o, q_o, stats_o, xt_o, bt_o, so_o = rest[:15]
    xbuf, bcbuf, state, rows_s, wd_s, hb = rest[15:]
    size = hid.shape[0]
    width = wz.shape[1]
    nst = wbc.shape[1] // 2
    pid = pl.program_id(0)

    @pl.when(pid == 0)
    def _():
        if c0:
            xbuf[0:TAIL, :] = xt_r[...]
            bcbuf[0:TAIL, :] = bt_r[...]
            state[...] = sin_r[...]
        else:
            xbuf[0:TAIL, :] = jnp.zeros((TAIL, width), F32)
            bcbuf[0:TAIL, :] = jnp.zeros((TAIL, 2 * nst), F32)
            state[...] = jnp.zeros_like(state)
        fill_rows(seg, rows_s, size)
        fill_params(width // psize, wdt, dtb_r, alog_r, dsk_r, wd_s, hb)

    rows = rows_s[:, pl.ds(pl.multiple_of((pid + c0) * size, size), size)]
    dtb, alog, skip = head_params(hb, width, psize)
    inputs = hid[...].astype(F32)
    rstd = lax.rsqrt(jnp.mean(inputs * inputs, axis=1, keepdims=True) + EPS)
    normed = (inputs * rstd * row_of(nw)).astype(BF)
    normed_o[...] = normed
    dtv = dot_nt(wd_s[...].astype(BF), normed) + dtb
    dtv_o[...] = dtv
    gate = dot(normed, wz[...])
    gate_o[...] = gate
    xraw = dot(normed, wx[...])
    bcraw = dot(normed, wbc[...])
    xraw_o[...] = xraw
    bcraw_o[...] = bcraw
    step, rate, decay, cum, ein, eout = decay_rows(dtv, alog, rows[1:2], rows[2:3])
    tcol = columns_of(step, cum, ein, eout, rows)

    xbuf[TAIL:, :] = xraw
    bcbuf[TAIL:, :] = bcraw
    xpre = row_of(cxb) + cx[3:4, :] * xraw
    bcpre = row_of(cbcb) + cbc[3:4, :] * bcraw
    for lag in (1, 2, 3):
        keep = tcol[:, 4 * HP + 3 + lag : 4 * HP + 4 + lag]
        xpre += cx[3 - lag : 4 - lag, :] * (xbuf[TAIL - lag : TAIL - lag + size, :] * keep)
        bcpre += cbc[3 - lag : 4 - lag, :] * (bcbuf[TAIL - lag : TAIL - lag + size, :] * keep)
    xbuf[0:TAIL, :] = xraw[size - TAIL :, :]
    bcbuf[0:TAIL, :] = bcraw[size - TAIL :, :]
    xpre_o[...] = xpre
    bcpre_o[...] = bcpre
    xs = xpre * sigmoid(xpre)
    bc = (bcpre * sigmoid(bcpre)).astype(BF)
    b_b = bc[:, :nst]
    c_b = bc[:, nst:]
    scaled = expand(tcol, 0, width, psize) * xs
    scaled_b = scaled.astype(BF)
    bias = jnp.where(chunk_mask(tcol[:, 4 * HP : 4 * HP + 1], rows[0:1, :]), 0.0, NEG)
    gram = dot_nt(c_b, b_b)
    state_b = state[...].astype(BF)
    st_o[0] = state_b
    cross = dot(c_b, state_b)
    ein_e = expand(tcol, 2 * HP, width, psize)
    ytiles = []
    for j, w in lane_tiles(width):
        lane = lax.broadcasted_iota(jnp.int32, (size, w), 1)
        tile = None
        for e in range(w // psize):
            h = j // psize + e
            dec = jnp.exp(tcol[:, HP + h : HP + h + 1] - cum[h : h + 1, :] + bias)
            got = dot((gram * dec).astype(BF), scaled_b[:, j : j + w])
            tile = got if tile is None else jnp.where(lane >= e * psize, got, tile)
        ytiles.append(tile)
    y = jnp.concatenate(ytiles, axis=1) if len(ytiles) > 1 else ytiles[0]
    y = y + ein_e * cross
    sent = (expand(tcol, 3 * HP, width, psize) * scaled).astype(BF)
    state[...] = ein_e[size - 1 : size, :] * state[...] + dot_tn(b_b, sent)
    y = y + skip * xs
    y_o[...] = y
    gated = y * (gate * sigmoid(gate))
    gno = dot_nt(og[...], wout[...])
    gno_o[...] = gno
    weighted = gated * row_of(gnw)
    sq = jnp.sum(gated * gated, axis=1, keepdims=True)
    gs = jnp.sum(gno * weighted, axis=1, keepdims=True)
    lane = lax.broadcasted_iota(jnp.int32, (size, 128), 1)
    stats_o[...] = jnp.where(lane == 0, sq, jnp.where(lane == 1, gs, 0.0)).T[0:HP, :]
    q_o[...] = dot(weighted.astype(BF), wout[...]).astype(BF)

    @pl.when(pid == pl.num_programs(0) - 1)
    def _():
        xt_o[...] = xbuf[0:TAIL, :]
        bt_o[...] = bcbuf[0:TAIL, :]
        so_o[...] = state[...]


class Pack:
    def __init__(self, dim, width, nst2, shards):
        self.shards = shards
        self.turned = (width // shards) % 16 != 0
        self.items = {}
        at = 0
        wo = (dim, width) if self.turned else (width, dim)
        sizes = [("wz", dim, width), ("wx", dim, width), ("wo", *wo), ("sm", 128, 128), ("wbc", dim, nst2), ("zs", 128, 128)]
        for name, rows, cols in sizes:
            if name == "wbc":
                self.zstart = at
            self.items[name] = (at, rows // shards, lane_tiles(cols))
            at += (rows // shards) * len(lane_tiles(cols))
        self.rows = at

    def partner(self, slot):
        bits = self.shards.bit_length() - 1
        return sum(1 << (bits - 1 - b) for b in range(bits) if (slot >> b) & 1)

    def pieces(self, name, me, slots):
        at, piece, tiles = self.items[name]
        for slot in slots:
            shard = me ^ self.partner(slot)
            for t, (j, w) in enumerate(tiles):
                yield (slot - slots[0]) * self.rows + at + t * piece, pl.ds(pl.multiple_of(shard * piece, 8), piece), piece, j, w

    def put(self, ref, name, value, me):
        for dst, src, piece, j, w in self.pieces(name, me, range(self.shards)):
            ref[dst : dst + piece, 0:w] = value[src, j : j + w].astype(BF)

    def take(self, ref, name, out, me, slots):
        for dst, src, piece, j, w in self.pieces(name, me, slots):
            out[src, j : j + w] = ref[dst : dst + piece, 0:w].astype(F32)


def tiles_of(value):
    out = []
    for j, w in lane_tiles(value.shape[1]):
        tile = value[:, j : j + w]
        if w < 128:
            tile = jnp.concatenate([tile, jnp.zeros((tile.shape[0], 128 - w), F32)], axis=1)
        out.append(tile)
    return out


def square(tiles):
    rows = sum(t.shape[0] for t in tiles)
    if rows < 128:
        tiles = tiles + [jnp.zeros((128 - rows, 128), F32)]
    return jnp.concatenate(tiles, axis=0)


def bwd_kernel(
    psize, di, c0, pack, hid, og, seg, normed_r, gate_r, xraw_r, xpre_r, bcraw_r, bcpre_r, dtv_r, y_r, gno_r, st_r, stats_r,
    wz, wx, wbc, wdt, cx, cbc, dtb_r, alog_r, dsk_r, gnw, me_r, *rest,
):
    size = hid.shape[0]
    width = wz.shape[1]
    nst = wbc.shape[1] // 2
    pid = pl.program_id(0)
    last = pl.num_programs(0) - 1
    nacc = 14
    final = pack is not None
    if final:
        carried = rest[:nacc]
        part_o, packed_o = rest[nacc : nacc + 2]
        accs = rest[nacc + 2 : 2 * nacc + 2]
        rows_s, wd_s, hb, sm_s, zs_s, turn_s = rest[2 * nacc + 2 :]
    else:
        part_o = rest[0]
        accs = rest[1 : nacc + 1]
        rows_s, wd_s, hb = rest[nacc + 1 :]
    awz, awx, awbc, awo, gwdt, gcx, gcbc, ggn, gnwp, gh, xbuf, bcbuf, ds, gcar = accs

    @pl.when(pid == 0)
    def _():
        fill_rows(seg, rows_s, size)
        fill_params(width // psize, wdt, dtb_r, alog_r, dsk_r, wd_s, hb)
        if final:
            for src, dst in zip(carried, accs):
                dst[...] = src[...]
        else:
            for ref in accs:
                ref[...] = jnp.zeros_like(ref)

    rows = rows_s[:, pl.ds(pl.multiple_of((c0 + last - pid) * size, size), size)]
    dtb, alog, skip = head_params(hb, width, psize)
    inputs = hid[...].astype(F32)
    in_rstd = lax.rsqrt(jnp.mean(inputs * inputs, axis=1, keepdims=True) + EPS)
    normed = normed_r[...]
    gate = gate_r[...]
    y = y_r[...]
    stats = stats_r[...]
    r_rstd = lax.rsqrt(stats[0:1] / di + EPS)
    r_beta = r_rstd * r_rstd * r_rstd * stats[1:2] / di
    step, rate, decay, cum, ein, eout = decay_rows(dtv_r[...], alog, rows[1:2], rows[2:3])
    pickr = lax.broadcasted_iota(jnp.int32, (HP, size), 0)
    tcol = columns_of(step, cum, ein, eout, rows, jnp.where(pickr == 0, r_rstd, r_beta))
    rstd = tcol[:, 6 * HP : 6 * HP + 1]
    beta = tcol[:, 6 * HP + 1 : 6 * HP + 2]

    sig = sigmoid(gate)
    act = gate * sig
    gated = y * act
    gno = gno_r[...]
    grs = gated * rstd
    gw = row_of(gnw)
    ggn[0:1, :] += jnp.sum(gno * grs, axis=0, keepdims=True)
    normed_out = (grs * gw).astype(BF)
    awo[...] += dot_tn(normed_out, og[...])
    ggated = rstd * (gno * gw) - gated * beta
    dy = ggated * act
    ggate_b = (ggated * y * (sig * (1.0 + gate * (1.0 - sig)))).astype(BF)

    xpre = xpre_r[...]
    xsig = sigmoid(xpre)
    xs = xpre * xsig
    step_e = expand(tcol, 0, width, psize)
    scaled = step_e * xs
    scaled_b = scaled.astype(BF)
    dy_b = dy.astype(BF)
    bcpre = bcpre_r[...]
    bcsig = sigmoid(bcpre)
    bc = (bcpre * bcsig).astype(BF)
    b_b = bc[:, :nst]
    c_b = bc[:, nst:]
    mask = chunk_mask(tcol[:, 4 * HP : 4 * HP + 1], rows[0:1, :])
    bias = jnp.where(mask, 0.0, NEG)
    gram = dot_nt(c_b, b_b)
    dgram = jnp.zeros((size, size), F32)
    dy_t = dy_b.T
    turned = []
    for j, w in lane_tiles(width):
        lane = lax.broadcasted_iota(jnp.int32, (size, w), 1)
        for e in range(w // psize):
            h = j // psize + e
            dec = jnp.exp(tcol[:, HP + h : HP + h + 1] - cum[h : h + 1, :] + bias)
            weights = (gram * dec).astype(BF)
            turned.append(dot(dy_t[h * psize : (h + 1) * psize, :], weights))
            mine = (lane >= e * psize) & (lane < (e + 1) * psize)
            left = jnp.where(mine, dy[:, j : j + w], 0.0).astype(BF)
            dgram += dot_nt(left, scaled_b[:, j : j + w]) * dec
    gsc = jnp.concatenate(turned, axis=0).T
    ds_b = ds[...].astype(BF)
    st_b = st_r[0]
    ein_e = expand(tcol, 2 * HP, width, psize)
    eout_e = expand(tcol, 3 * HP, width, psize)
    gsc += eout_e * dot(b_b, ds_b)
    sent = (eout_e * scaled).astype(BF)
    seen = (ein_e * dy).astype(BF)
    dgram_b = dgram.astype(BF)
    gb = dot_tn(dgram_b, c_b) + dot_nt(sent, ds_b)
    gc = dot(dgram_b, b_b) + dot_nt(seen, st_b)
    ds[...] = ein_e[size - 1 : size, :] * ds[...] + dot_tn(c_b, seen)

    y_ns = y - skip * xs
    sums = head_sums(dy_b.astype(F32) * y_ns - scaled_b.astype(F32) * gsc, 0, psize)
    sums += head_sums(gsc * xs, HP, psize) + head_sums(dy * xs, 2 * HP, psize)
    sums = sums.T
    gcum = sums[0:HP, :]
    gdecay = rows_dot(gcum, jnp.where(mask, 1.0, 0.0).astype(BF)) + gcar[:, 0:1] * rows[3:4, :]
    gcar[:, 0:1] = gdecay[:, 0:1]
    gstep = sums[HP : 2 * HP, :] + gdecay * rate
    gdtv = gstep * sigmoid(dtv_r[...])
    gh[:, 0:1] += jnp.sum(gdecay * decay, axis=1, keepdims=True)
    gh[:, 1:2] += jnp.sum(gdtv, axis=1, keepdims=True)
    gh[:, 2:3] += jnp.sum(sums[2 * HP : 3 * HP, :], axis=1, keepdims=True)
    gwdt[...] += dot(gdtv.astype(BF), normed)
    gdt_col = columns_of(gdtv)[:, 0:HP].astype(BF)

    gxp = (dy * skip + gsc * step_e) * (xsig * (1.0 + xpre * (1.0 - xsig)))
    xraw = xraw_r[...]
    bcraw = bcraw_r[...]
    gbp = jnp.concatenate([gb, gc], axis=1) * (bcsig * (1.0 + bcpre * (1.0 - bcsig)))
    xbuf[0:size, :] = gxp
    bcbuf[0:size, :] = gbp
    gx = cx[3:4, :] * gxp
    gbc = cbc[3:4, :] * gbp
    gcx[3:4, :] += jnp.sum(gxp * xraw, axis=0, keepdims=True)
    gcbc[3:4, :] += jnp.sum(gbp * bcraw, axis=0, keepdims=True)
    gcx[4:5, :] += jnp.sum(gxp, axis=0, keepdims=True)
    gcbc[4:5, :] += jnp.sum(gbp, axis=0, keepdims=True)
    for lag in (1, 2, 3):
        keep = tcol[:, 4 * HP + 6 + lag : 4 * HP + 7 + lag]
        moved = xbuf[lag : lag + size, :] * keep
        gx += cx[3 - lag : 4 - lag, :] * moved
        gcx[3 - lag : 4 - lag, :] += jnp.sum(moved * xraw, axis=0, keepdims=True)
        moved = bcbuf[lag : lag + size, :] * keep
        gbc += cbc[3 - lag : 4 - lag, :] * moved
        gcbc[3 - lag : 4 - lag, :] += jnp.sum(moved * bcraw, axis=0, keepdims=True)
    xbuf[size:, :] = gxp[0:TAIL, :]
    bcbuf[size:, :] = gbp[0:TAIL, :]
    gx_b = gx.astype(BF)
    gbc_b = gbc.astype(BF)
    nt = normed.T
    awz[...] += dot(nt, ggate_b)
    awx[...] += dot(nt, gx_b)
    awbc[...] += dot(nt, gbc_b)
    part = dot_nt(ggate_b, wz[...]) + dot_nt(gx_b, wx[...]) + dot_nt(gbc_b, wbc[...]) + dot(gdt_col, wd_s[...].astype(BF))
    part_o[...] = part.astype(BF)
    gnwp[0:1, :] += jnp.sum(part * (inputs * in_rstd), axis=0, keepdims=True)

    if final:

        @pl.when(pid == last)
        def _():
            if width % 128:
                packed_o[...] = jnp.zeros_like(packed_o)
            me = me_r[0]
            pack.put(packed_o, "wz", awz, me)
            pack.put(packed_o, "wx", awx, me)
            if pack.turned:
                turn_s[...] = awo[...].T
                pack.put(packed_o, "wo", turn_s, me)
            else:
                pack.put(packed_o, "wo", awo, me)
            pack.put(packed_o, "wbc", awbc, me)
            heads_t = square([gh[...]]).T[0:HP, :]
            sm_s[...] = square(tiles_of(gwdt[...]) + tiles_of(gcx[...]) + tiles_of(ggn[...]) + [heads_t])
            pack.put(packed_o, "sm", sm_s, me)
            zs_s[...] = square(tiles_of(gcbc[...]) + tiles_of(gnwp[...]))
            pack.put(packed_o, "zs", zs_s, me)


def unpack_kernel(
    pack, heads, me_r, packed, other,
    gnw_o, gwz_o, gwx_o, gwbc_o, gwdt_o, gcx_o, gcxb_o, gcbc_o, gcbcb_o, gdtb_o, gal_o, gds_o, ggn_o, gwo_o,
    sm, zs, turn_s,
):
    me = me_r[0]
    half = pack.shards // 2
    for ref, slots in ((packed, range(half)), (other, range(half, 2 * half))):
        pack.take(ref, "wz", gwz_o, me, slots)
        pack.take(ref, "wx", gwx_o, me, slots)
        pack.take(ref, "wo", turn_s if pack.turned else gwo_o, me, slots)
        pack.take(ref, "wbc", gwbc_o, me, slots)
        pack.take(ref, "sm", sm, me, slots)
        pack.take(ref, "zs", zs, me, slots)
    if pack.turned:
        gwo_o[...] = turn_s[...].T
    dim, width = gwz_o.shape

    def wide(ref, at, total):
        tiles = [ref[at + 8 * t : at + 8 * t + 8, 0:w] for t, (j, w) in enumerate(lane_tiles(total))]
        return jnp.concatenate(tiles, axis=1) if len(tiles) > 1 else tiles[0], at + 8 * len(tiles)

    gwdt, at = wide(sm, 0, dim)
    gcx, at = wide(sm, at, width)
    ggn, at = wide(sm, at, width)
    gh = sm[at : at + 8, :]
    gcbc, at = wide(zs, 0, gcbc_o.shape[1])
    gnw, at = wide(zs, at, dim)
    gwdt_o[...] = gwdt[0:heads]
    gcx_o[...] = gcx[0:4]
    gcxb_o[...] = gcx[4]
    gcbc_o[...] = gcbc[0:4]
    gcbcb_o[...] = gcbc[4]
    gnw_o[...] = gnw[0]
    ggn_o[...] = ggn[0]
    gal_o[...] = gh[0, 0:heads]
    gdtb_o[...] = gh[1, 0:heads]
    gds_o[...] = gh[2, 0:heads]


def block_kernel(di, hid, mixed_r, stats_r, *rest):
    block_o = rest[-1]
    size = hid.shape[0]
    col = columns_of(lax.rsqrt(stats_r[...] / di + EPS))[:, 0:1]
    block_o[...] = (hid[...].astype(F32) + col * mixed_r[...].astype(F32)).astype(BF)


def ingrad_kernel(hid, og, grad_r, nw, *rest):
    ingrad_o = rest[-1]
    inputs = hid[...].astype(F32)
    rstd = lax.rsqrt(jnp.mean(inputs * inputs, axis=1, keepdims=True) + EPS)
    gn = grad_r[...].astype(F32) * row_of(nw)
    mean = jnp.mean(gn * inputs, axis=1, keepdims=True)
    ingrad_o[...] = og[...].astype(F32) + rstd * gn - inputs * (rstd * rstd * rstd * mean)


def swap(value, axis, count, mask):
    return lax.ppermute(value, axis, [(i, i ^ mask) for i in range(count)])


def plus(a, b):
    return (a.astype(F32) + b.astype(F32)).astype(a.dtype)


def local(
    hidden_in, segment_ids, norm_weight, w_z, w_x, w_bc, w_dt, conv_x, conv_x_bias, conv_bc, conv_bc_bias,
    dt_bias, a_log, d_skip, gate_norm_weight, w_out, out_grad, n_tensor, n_dp,
):
    total = segment_ids.shape[1]
    dim = hidden_in.shape[1]
    heads = dt_bias.shape[0]
    width = w_z.shape[1]
    psize = width // heads
    nst = w_bc.shape[1] // 2
    di = width * n_tensor
    size = CHUNK
    half = total // 2
    nh = half // size
    wdt = w_dt.T
    me = jnp.reshape(lax.axis_index("dp"), (1,)).astype(jnp.int32)

    def whole(a):
        return pl.BlockSpec(a.shape, lambda i: (0,) * len(a.shape))

    def out(shape, dt):
        return jax.ShapeDtypeStruct(shape, dt)

    def cost(us):
        return pl.CostEstimate(flops=int(us * 1.0e9), bytes_accessed=int(us * 3.0e6), transcendentals=0)

    kept = [(TAIL, width), (TAIL, 2 * nst), (nst, width)]
    params = [pltpu.VMEM((16, total), F32), pltpu.VMEM((HP, dim), F32), pltpu.VMEM((HP, 128), F32)]

    def full(s):
        return pl.BlockSpec(s, lambda i: (0,) * len(s))

    def forward(part, carry):
        c0 = part * nh

        def tok(w):
            return pl.BlockSpec((size, w), lambda i: (i, 0))

        def src(w):
            return pl.BlockSpec((size, w), lambda i: (i + c0, 0))

        def rowf(h):
            return pl.BlockSpec((h, size), lambda i: (0, i))

        fixed = (
            segment_ids, norm_weight, w_z, w_x, w_bc, wdt, conv_x, conv_x_bias, conv_bc, conv_bc_bias, dt_bias,
            a_log, d_skip, gate_norm_weight, w_out,
        ) + carry
        return pl.pallas_call(
            functools.partial(fwd_kernel, psize, c0),
            grid=(nh,),
            in_specs=[src(dim), src(dim)] + [whole(a) for a in fixed],
            out_specs=[
                tok(dim), tok(width), tok(width), tok(width), tok(2 * nst), tok(2 * nst), rowf(HP), tok(width), tok(width),
                pl.BlockSpec((1, nst, width), lambda i: (i, 0, 0)), tok(dim), rowf(HP),
            ] + [full(a) for a in kept],
            out_shape=[
                out((half, dim), BF), out((half, width), F32), out((half, width), F32), out((half, width), F32),
                out((half, 2 * nst), F32), out((half, 2 * nst), F32), out((HP, half), F32), out((half, width), F32),
                out((half, width), F32), out((nh, nst, width), BF), out((half, dim), BF), out((HP, half), F32),
            ] + [out(a, F32) for a in kept],
            scratch_shapes=[
                pltpu.VMEM((size + TAIL, width), F32), pltpu.VMEM((size + TAIL, 2 * nst), F32), pltpu.VMEM((nst, width), F32),
            ] + params,
            cost_estimate=cost(9),
            name="fwd",
        )(hidden_in, out_grad, *fixed)

    pack = Pack(dim, width, 2 * nst, n_dp)
    accs = [
        (dim, width), (dim, width), (dim, 2 * nst), (width, dim), (HP, dim), (HP, width), (HP, 2 * nst), (HP, width), (HP, dim),
        (HP, 128), (size + TAIL, width), (size + TAIL, 2 * nst), (nst, width), (HP, 128),
    ]

    def backward(part, saved, stats, carried):
        c0 = part * nh
        final = carried is not None

        def tok(w):
            return pl.BlockSpec((size, w), lambda i: (nh - 1 - i, 0))

        def src(w):
            return pl.BlockSpec((size, w), lambda i: (c0 + nh - 1 - i, 0))

        def rowb(h):
            return pl.BlockSpec((h, size), lambda i: (0, nh - 1 - i))

        fixed = (w_z, w_x, w_bc, wdt, conv_x, conv_bc, dt_bias, a_log, d_skip, gate_norm_weight)
        held = tuple(carried) if final else ()
        if final:
            shapes = [out((half, dim), BF), out((pack.shards * pack.rows, 128), BF)]
            specs = [tok(dim), full((pack.shards * pack.rows, 128))]
            turn = (dim, width) if pack.turned else (HP, 128)
            scratch = [pltpu.VMEM(s, F32) for s in accs]
            extra = [pltpu.VMEM((128, 128), F32), pltpu.VMEM((128, 128), F32), pltpu.VMEM(turn, F32)]
        else:
            shapes = [out((half, dim), BF)] + [out(s, F32) for s in accs]
            specs = [tok(dim)] + [full(s) for s in accs]
            scratch = []
            extra = []
        return pl.pallas_call(
            functools.partial(bwd_kernel, psize, di, c0, pack if final else None),
            grid=(nh,),
            in_specs=[
                src(dim), src(dim), whole(segment_ids), tok(dim), tok(width), tok(width), tok(width), tok(2 * nst),
                tok(2 * nst), rowb(HP), tok(width), tok(width),
                pl.BlockSpec((1, nst, width), lambda i: (nh - 1 - i, 0, 0)), rowb(HP),
            ] + [whole(a) for a in fixed] + [pl.BlockSpec(memory_space=pltpu.SMEM)] + [whole(a) for a in held],
            out_specs=specs,
            out_shape=shapes,
            scratch_shapes=scratch + params + extra,
            cost_estimate=cost(15),
            name="bwd",
        )(hidden_in, out_grad, segment_ids, *saved, stats, *fixed, me, *held)

    stride = n_tensor // 4
    place = lax.axis_index("tensor") // stride
    inner = (place == 1) | (place == 2)

    def outer(value):
        return lax.ppermute(value, "tensor", [(z * stride + j, (z ^ 1) * stride + j) for z in range(4) for j in range(stride)])

    def middle(value):
        return lax.ppermute(value, "tensor", [(z * stride + j, (3 - z) * stride + j) for z in (1, 2) for j in range(stride)])

    def joined(value):
        mask = 1
        while mask < stride:
            value = plus(value, swap(value, "tensor", n_tensor, mask))
            mask *= 2
        return value

    def summed(value):
        mask = 1
        while mask < n_tensor:
            value = value + swap(value, "tensor", n_tensor, mask)
            mask *= 2
        return value

    fa = forward(0, ())
    q0 = joined(fa[10])
    r0 = outer(q0)
    fb = forward(1, tuple(fa[12:15]))
    q1 = joined(fb[10])
    stats = summed(jnp.concatenate([fa[11], fb[11]], axis=1))
    stats_a, stats_b = stats[:, :half], stats[:, half:]
    a0 = plus(q0, r0)
    stats_b, a0 = lax.optimization_barrier((stats_b, a0))
    r1 = outer(q1)
    m0 = middle(a0)
    b1 = backward(1, fb[:10], stats_b, None)
    p1 = joined(b1[0])
    t0 = plus(a0, m0)
    a1 = plus(q1, r1)
    stats_a, t0, a1 = lax.optimization_barrier((stats_a, t0, a1))
    r2 = outer(jnp.where(inner, t0, p1))
    m1 = middle(a1)
    p0, packed = backward(0, fa[:10], stats_a, b1[1:])
    p0 = joined(p0)
    mixed0 = jnp.where(inner, t0, r2)
    ap1 = plus(p1, r2)
    t1 = plus(a1, m1)
    r3 = outer(jnp.where(inner, t1, p0))
    mp1 = middle(ap1)
    mixed1 = jnp.where(inner, t1, r3)
    ap0 = plus(p0, r3)
    tp1 = plus(ap1, mp1)
    r4 = outer(tp1)
    mp0 = middle(ap0)
    grad1 = jnp.where(inner, tp1, r4)
    tp0 = plus(ap0, mp0)
    r5 = outer(tp0)
    grad0 = jnp.where(inner, tp0, r5)

    masks = []
    mask = 1
    while mask < n_dp:
        masks.append(mask)
        mask *= 2
    buf = packed
    for mask in masks:
        rows = buf.shape[0] // 2
        buf = plus(buf[:rows], swap(buf[rows:], "dp", n_dp, mask))
    zpart = summed(buf[pack.zstart :].astype(F32)).astype(BF)
    buf = jnp.concatenate([buf[: pack.zstart], zpart])
    for mask in masks[:0:-1]:
        buf = jnp.concatenate([buf, swap(buf, "dp", n_dp, mask)])
    other = swap(buf, "dp", n_dp, masks[0])

    def blk(w, c0=0):
        return pl.BlockSpec((size, w), lambda i: (i + c0, 0))

    def written(part, name, kernel, dt, args, specs, held):
        return pl.pallas_call(
            kernel,
            grid=(nh,),
            in_specs=specs + ([pl.BlockSpec(memory_space=pl.ANY)] if part else []),
            out_specs=blk(dim, (1 - part) * nh),
            out_shape=out((total, dim), dt),
            input_output_aliases={len(args): 0} if part else {},
            cost_estimate=cost(1),
            name=name,
        )(*args, *held)

    def block(part, mixed, st, *held):
        specs = [blk(dim, (1 - part) * nh), blk(dim), pl.BlockSpec((HP, size), lambda i: (0, i))]
        return written(part, "block", functools.partial(block_kernel, di), BF, (hidden_in, mixed, st), specs, held)

    def ingrad(part, grad, *held):
        specs = [blk(dim, (1 - part) * nh), blk(dim, (1 - part) * nh), blk(dim), whole(norm_weight)]
        return written(part, "ingrad", ingrad_kernel, F32, (hidden_in, out_grad, grad, norm_weight), specs, held)

    block_out = block(1, mixed0, stats_a, block(0, mixed1, stats_b))
    in_grad = ingrad(1, grad0, ingrad(0, grad1))
    grads = pl.pallas_call(
        functools.partial(unpack_kernel, pack, heads),
        out_shape=[
            out((dim,), F32), out((dim, width), F32), out((dim, width), F32), out((dim, 2 * nst), F32), out((heads, dim), F32),
            out((4, width), F32), out((width,), F32), out((4, 2 * nst), F32), out((2 * nst,), F32), out((heads,), F32),
            out((heads,), F32), out((heads,), F32), out((width,), F32), out((width, dim), F32),
        ],
        in_specs=[pl.BlockSpec(memory_space=pltpu.SMEM)] + [pl.BlockSpec(memory_space=pltpu.VMEM)] * 2,
        scratch_shapes=[
            pltpu.VMEM((128, 128), F32), pltpu.VMEM((128, 128), F32), pltpu.VMEM((dim, width) if pack.turned else (HP, 128), F32),
        ],
        cost_estimate=cost(3),
        name="unpack",
    )(me, buf, other)
    return (block_out, in_grad, *grads[:4], grads[4].T, *grads[5:])

def solution(mesh):
    t = P(None, "tensor")
    return jax.shard_map(
        functools.partial(local, n_tensor=mesh.shape["tensor"], n_dp=mesh.shape["dp"]),
        mesh=mesh,
        in_specs=(
            P("dp", None), P("dp", None), P(), t, t, P(), t, t, P("tensor"), P(), P(),
            P("tensor"), P("tensor"), P("tensor"), P("tensor"), P("tensor", None), P("dp", None),
        ),
        out_specs=(
            P("dp", None), P("dp", None), P(), t, t, P(), t, t, P("tensor"), P(), P(),
            P("tensor"), P("tensor"), P("tensor"), P("tensor"), P("tensor", None),
        ),
        check_vma=False,
    )
```

```python
import functools

import jax
import jax.numpy as jnp
from jax import lax
from jax.experimental import pallas as pl
from jax.experimental.pallas import tpu as pltpu
from jax.sharding import PartitionSpec as P

EPS = 1e-05
HIGH = lax.Precision.HIGHEST
F32 = jnp.float32
BF = jnp.bfloat16
NEG = -1e30
CHUNK = 256
HP = 8
TAIL = 8


def dot(a, b, prec=None):
    return lax.dot_general(a, b, (((1,), (0,)), ((), ())), precision=prec, preferred_element_type=F32)


def dot_nt(a, b, prec=None):
    return lax.dot_general(a, b, (((1,), (1,)), ((), ())), precision=prec, preferred_element_type=F32)


def dot_tn(a, b, prec=None):
    return lax.dot_general(a, b, (((0,), (0,)), ((), ())), precision=prec, preferred_element_type=F32)


def sigmoid(v):
    return 0.5 * jnp.tanh(0.5 * v) + 0.5


def split3(v):
    a = v.astype(BF)
    left = v - a.astype(F32)
    b = left.astype(BF)
    return jnp.concatenate([a.astype(F32), b.astype(F32), left - b.astype(F32)], axis=0).astype(BF)


def rows_dot(v, ones):
    got = dot(split3(v), ones)
    n = v.shape[0]
    return got[0:n] + got[n : 2 * n] + got[2 * n : 3 * n]


def head_sums(v, base, psize):
    width = v.shape[1]
    unit = lax.broadcasted_iota(jnp.int32, (width, 128), 0)
    lane = lax.broadcasted_iota(jnp.int32, (width, 128), 1) - base
    mark = jnp.where((unit >= lane * psize) & (unit < (lane + 1) * psize), 1.0, 0.0).astype(BF)
    big = v.astype(BF)
    return dot(big, mark) + dot((v - big.astype(F32)).astype(BF), mark)


def softplus(v):
    return jnp.maximum(v, 0.0) + jnp.log1p(jnp.exp(-jnp.abs(v)))


def lane_tiles(width):
    return [(j, min(128, width - j)) for j in range(0, width, 128)]


def expand(cols, base, width, psize):
    rows = cols.shape[0]
    out = []
    for j, w in lane_tiles(width):
        first = base + j // psize
        tile = jnp.broadcast_to(cols[:, first : first + 1], (rows, w))
        lane = lax.broadcasted_iota(jnp.int32, (rows, w), 1)
        for extra in range(1, w // psize):
            tile = jnp.where(
                lane >= extra * psize,
                jnp.broadcast_to(cols[:, first + extra : first + extra + 1], (rows, w)),
                tile,
            )
        out.append(tile)
    return jnp.concatenate(out, axis=1) if len(out) > 1 else out[0]


def chunk_mask(segcol, segrow):
    size = segcol.shape[0]
    row = lax.broadcasted_iota(jnp.int32, (size, size), 0)
    col = lax.broadcasted_iota(jnp.int32, (size, size), 1)
    return (row >= col) & (segcol == segrow)


def decay_rows(dtv, alog, inm, outm):
    size = dtv.shape[1]
    step = softplus(dtv)
    rate = -jnp.exp(alog)
    decay = step * rate
    row = lax.broadcasted_iota(jnp.int32, (size, size), 0)
    col = lax.broadcasted_iota(jnp.int32, (size, size), 1)
    cum = rows_dot(decay, jnp.where(row <= col, 1.0, 0.0).astype(BF))
    end = cum[:, size - 1 : size]
    ein = jnp.exp(cum) * inm
    eout = jnp.exp(end - cum) * outm
    return step, rate, decay, cum, ein, eout


def columns_of(*parts):
    stack = jnp.concatenate(parts, axis=0)
    pad = 128 - stack.shape[0]
    if pad:
        stack = jnp.concatenate([stack, jnp.zeros((pad, stack.shape[1]), F32)], axis=0)
    return stack.T


def fill_rows(seg_ref, rows_s, size):
    total = seg_ref.shape[1]
    seg = seg_ref[...].astype(F32)
    wide = jnp.broadcast_to(seg, (8, total))
    lane = lax.broadcasted_iota(jnp.int32, (8, total), 1)
    rows_s[...] = jnp.zeros_like(rows_s)
    rows_s[0:1, :] = seg
    for lag in (1, 2, 3):
        back = (pltpu.roll(wide, lag, 1) == wide) & (lane >= lag)
        rows_s[3 + lag : 4 + lag, :] = jnp.where(back, 1.0, 0.0)[0:1]
        ahead = (pltpu.roll(wide, total - lag, 1) == wide) & (lane < total - lag)
        rows_s[6 + lag : 7 + lag, :] = jnp.where(ahead, 1.0, 0.0)[0:1]
    for start in range(0, total, size):
        end = start + size
        part = seg[:, start:end]
        if start:
            rows_s[1:2, start:end] = jnp.where(part == seg[:, start - 1 : start], 1.0, 0.0)
        rows_s[2:3, start:end] = jnp.where(part == seg[:, end - 1 : end], 1.0, 0.0)
        if end < total:
            rows_s[3:4, start:end] = jnp.where(part == seg[:, end : end + 1], 1.0, 0.0)


def row_of(ref):
    return ref[...].reshape(1, -1)


def fill_params(heads, wdt, dtb, alog, dsk, wd_s, hb):
    wd_s[...] = jnp.zeros_like(wd_s)
    wd_s[0:heads, :] = wdt[...].astype(F32)
    hb[...] = jnp.zeros_like(hb)
    for i, ref in enumerate((dtb, alog, dsk)):
        hb[i : i + 1, 0:heads] = row_of(ref)


def head_params(hb, width, psize):
    rows = hb[...]
    cols = square([rows]).T
    skip = expand(rows, 0, width, psize)[2:3, :]
    return cols[0:HP, 0:1], cols[0:HP, 1:2], skip


def fwd_kernel(
    psize, c0, hid, og, seg, nw, wz, wx, wbc, wdt, cx, cxb, cbc, cbcb, dtb_r, alog_r, dsk_r, gnw, wout, *rest,
):
    if c0:
        xt_r, bt_r, sin_r = rest[:3]
        rest = rest[3:]
    normed_o, gate_o, xraw_o, xpre_o, bcraw_o, bcpre_o, dtv_o, y_o, gno_o, st_o, q_o, stats_o, xt_o, bt_o, so_o = rest[:15]
    xbuf, bcbuf, state, rows_s, wd_s, hb = rest[15:]
    size = hid.shape[0]
    width = wz.shape[1]
    nst = wbc.shape[1] // 2
    pid = pl.program_id(0)

    @pl.when(pid == 0)
    def _():
        if c0:
            xbuf[0:TAIL, :] = xt_r[...]
            bcbuf[0:TAIL, :] = bt_r[...]
            state[...] = sin_r[...]
        else:
            xbuf[0:TAIL, :] = jnp.zeros((TAIL, width), F32)
            bcbuf[0:TAIL, :] = jnp.zeros((TAIL, 2 * nst), F32)
            state[...] = jnp.zeros_like(state)
        fill_rows(seg, rows_s, size)
        fill_params(width // psize, wdt, dtb_r, alog_r, dsk_r, wd_s, hb)

    rows = rows_s[:, pl.ds(pl.multiple_of((pid + c0) * size, size), size)]
    dtb, alog, skip = head_params(hb, width, psize)
    inputs = hid[...].astype(F32)
    rstd = lax.rsqrt(jnp.mean(inputs * inputs, axis=1, keepdims=True) + EPS)
    normed = (inputs * rstd * row_of(nw)).astype(BF)
    normed_o[...] = normed
    dtv = dot_nt(wd_s[...].astype(BF), normed) + dtb
    dtv_o[...] = dtv
    gate = dot(normed, wz[...])
    gate_o[...] = gate
    xraw = dot(normed, wx[...])
    bcraw = dot(normed, wbc[...])
    xraw_o[...] = xraw
    bcraw_o[...] = bcraw
    step, rate, decay, cum, ein, eout = decay_rows(dtv, alog, rows[1:2], rows[2:3])
    tcol = columns_of(step, cum, ein, eout, rows)

    xbuf[TAIL:, :] = xraw
    bcbuf[TAIL:, :] = bcraw
    xpre = row_of(cxb) + cx[3:4, :] * xraw
    bcpre = row_of(cbcb) + cbc[3:4, :] * bcraw
    for lag in (1, 2, 3):
        keep = tcol[:, 4 * HP + 3 + lag : 4 * HP + 4 + lag]
        xpre += cx[3 - lag : 4 - lag, :] * (xbuf[TAIL - lag : TAIL - lag + size, :] * keep)
        bcpre += cbc[3 - lag : 4 - lag, :] * (bcbuf[TAIL - lag : TAIL - lag + size, :] * keep)
    xbuf[0:TAIL, :] = xraw[size - TAIL :, :]
    bcbuf[0:TAIL, :] = bcraw[size - TAIL :, :]
    xpre_o[...] = xpre
    bcpre_o[...] = bcpre
    xs = xpre * sigmoid(xpre)
    bc = (bcpre * sigmoid(bcpre)).astype(BF)
    b_b = bc[:, :nst]
    c_b = bc[:, nst:]
    scaled = expand(tcol, 0, width, psize) * xs
    scaled_b = scaled.astype(BF)
    bias = jnp.where(chunk_mask(tcol[:, 4 * HP : 4 * HP + 1], rows[0:1, :]), 0.0, NEG)
    gram = dot_nt(c_b, b_b)
    state_b = state[...].astype(BF)
    st_o[0] = state_b
    cross = dot(c_b, state_b)
    ein_e = expand(tcol, 2 * HP, width, psize)
    ytiles = []
    for j, w in lane_tiles(width):
        lane = lax.broadcasted_iota(jnp.int32, (size, w), 1)
        tile = None
        for e in range(w // psize):
            h = j // psize + e
            dec = jnp.exp(tcol[:, HP + h : HP + h + 1] - cum[h : h + 1, :] + bias)
            got = dot((gram * dec).astype(BF), scaled_b[:, j : j + w])
            tile = got if tile is None else jnp.where(lane >= e * psize, got, tile)
        ytiles.append(tile)
    y = jnp.concatenate(ytiles, axis=1) if len(ytiles) > 1 else ytiles[0]
    y = y + ein_e * cross
    sent = (expand(tcol, 3 * HP, width, psize) * scaled).astype(BF)
    state[...] = ein_e[size - 1 : size, :] * state[...] + dot_tn(b_b, sent)
    y = y + skip * xs
    y_o[...] = y
    gated = y * (gate * sigmoid(gate))
    gno = dot_nt(og[...], wout[...])
    gno_o[...] = gno
    weighted = gated * row_of(gnw)
    sq = jnp.sum(gated * gated, axis=1, keepdims=True)
    gs = jnp.sum(gno * weighted, axis=1, keepdims=True)
    lane = lax.broadcasted_iota(jnp.int32, (size, 128), 1)
    stats_o[...] = jnp.where(lane == 0, sq, jnp.where(lane == 1, gs, 0.0)).T[0:HP, :]
    q_o[...] = dot(weighted.astype(BF), wout[...]).astype(BF)

    @pl.when(pid == pl.num_programs(0) - 1)
    def _():
        xt_o[...] = xbuf[0:TAIL, :]
        bt_o[...] = bcbuf[0:TAIL, :]
        so_o[...] = state[...]


class Pack:
    def __init__(self, dim, width, nst2, shards):
        self.shards = shards
        self.turned = (width // shards) % 16 != 0
        self.items = {}
        at = 0
        wo = (dim, width) if self.turned else (width, dim)
        sizes = [("wz", dim, width), ("wx", dim, width), ("wo", *wo), ("sm", 128, 128), ("wbc", dim, nst2), ("zs", 128, 128)]
        for name, rows, cols in sizes:
            if name == "wbc":
                self.zstart = at
            self.items[name] = (at, rows // shards, lane_tiles(cols))
            at += (rows // shards) * len(lane_tiles(cols))
        self.rows = at

    def partner(self, slot):
        bits = self.shards.bit_length() - 1
        return sum(1 << (bits - 1 - b) for b in range(bits) if (slot >> b) & 1)

    def pieces(self, name, me, slots):
        at, piece, tiles = self.items[name]
        for slot in slots:
            shard = me ^ self.partner(slot)
            for t, (j, w) in enumerate(tiles):
                yield (slot - slots[0]) * self.rows + at + t * piece, pl.ds(pl.multiple_of(shard * piece, 8), piece), piece, j, w

    def put(self, ref, name, value, me):
        for dst, src, piece, j, w in self.pieces(name, me, range(self.shards)):
            ref[dst : dst + piece, 0:w] = value[src, j : j + w].astype(BF)

    def take(self, ref, name, out, me, slots):
        for dst, src, piece, j, w in self.pieces(name, me, slots):
            out[src, j : j + w] = ref[dst : dst + piece, 0:w].astype(F32)


def tiles_of(value):
    out = []
    for j, w in lane_tiles(value.shape[1]):
        tile = value[:, j : j + w]
        if w < 128:
            tile = jnp.concatenate([tile, jnp.zeros((tile.shape[0], 128 - w), F32)], axis=1)
        out.append(tile)
    return out


def square(tiles):
    rows = sum(t.shape[0] for t in tiles)
    if rows < 128:
        tiles = tiles + [jnp.zeros((128 - rows, 128), F32)]
    return jnp.concatenate(tiles, axis=0)


def bwd_kernel(
    psize, di, c0, pack, hid, og, seg, normed_r, gate_r, xraw_r, xpre_r, bcraw_r, bcpre_r, dtv_r, y_r, gno_r, st_r, stats_r,
    wz, wx, wbc, wdt, cx, cbc, dtb_r, alog_r, dsk_r, gnw, me_r, *rest,
):
    size = hid.shape[0]
    width = wz.shape[1]
    nst = wbc.shape[1] // 2
    pid = pl.program_id(0)
    last = pl.num_programs(0) - 1
    nacc = 14
    final = pack is not None
    if final:
        carried = rest[:nacc]
        part_o, packed_o = rest[nacc : nacc + 2]
        accs = rest[nacc + 2 : 2 * nacc + 2]
        rows_s, wd_s, hb, sm_s, zs_s, turn_s = rest[2 * nacc + 2 :]
    else:
        part_o = rest[0]
        accs = rest[1 : nacc + 1]
        rows_s, wd_s, hb = rest[nacc + 1 :]
    awz, awx, awbc, awo, gwdt, gcx, gcbc, ggn, gnwp, gh, xbuf, bcbuf, ds, gcar = accs

    @pl.when(pid == 0)
    def _():
        fill_rows(seg, rows_s, size)
        fill_params(width // psize, wdt, dtb_r, alog_r, dsk_r, wd_s, hb)
        if final:
            for src, dst in zip(carried, accs):
                dst[...] = src[...]
        else:
            for ref in accs:
                ref[...] = jnp.zeros_like(ref)

    rows = rows_s[:, pl.ds(pl.multiple_of((c0 + last - pid) * size, size), size)]
    dtb, alog, skip = head_params(hb, width, psize)
    inputs = hid[...].astype(F32)
    in_rstd = lax.rsqrt(jnp.mean(inputs * inputs, axis=1, keepdims=True) + EPS)
    normed = normed_r[...]
    gate = gate_r[...]
    y = y_r[...]
    stats = stats_r[...]
    r_rstd = lax.rsqrt(stats[0:1] / di + EPS)
    r_beta = r_rstd * r_rstd * r_rstd * stats[1:2] / di
    step, rate, decay, cum, ein, eout = decay_rows(dtv_r[...], alog, rows[1:2], rows[2:3])
    pickr = lax.broadcasted_iota(jnp.int32, (HP, size), 0)
    tcol = columns_of(step, cum, ein, eout, rows, jnp.where(pickr == 0, r_rstd, r_beta))
    rstd = tcol[:, 6 * HP : 6 * HP + 1]
    beta = tcol[:, 6 * HP + 1 : 6 * HP + 2]

    sig = sigmoid(gate)
    act = gate * sig
    gated = y * act
    gno = gno_r[...]
    grs = gated * rstd
    gw = row_of(gnw)
    ggn[0:1, :] += jnp.sum(gno * grs, axis=0, keepdims=True)
    normed_out = (grs * gw).astype(BF)
    awo[...] += dot_tn(normed_out, og[...])
    ggated = rstd * (gno * gw) - gated * beta
    dy = ggated * act
    ggate_b = (ggated * y * (sig * (1.0 + gate * (1.0 - sig)))).astype(BF)

    xpre = xpre_r[...]
    xsig = sigmoid(xpre)
    xs = xpre * xsig
    step_e = expand(tcol, 0, width, psize)
    scaled = step_e * xs
    scaled_b = scaled.astype(BF)
    dy_b = dy.astype(BF)
    bcpre = bcpre_r[...]
    bcsig = sigmoid(bcpre)
    bc = (bcpre * bcsig).astype(BF)
    b_b = bc[:, :nst]
    c_b = bc[:, nst:]
    mask = chunk_mask(tcol[:, 4 * HP : 4 * HP + 1], rows[0:1, :])
    bias = jnp.where(mask, 0.0, NEG)
    gram = dot_nt(c_b, b_b)
    dgram = jnp.zeros((size, size), F32)
    dy_t = dy_b.T
    turned = []
    for j, w in lane_tiles(width):
        lane = lax.broadcasted_iota(jnp.int32, (size, w), 1)
        for e in range(w // psize):
            h = j // psize + e
            dec = jnp.exp(tcol[:, HP + h : HP + h + 1] - cum[h : h + 1, :] + bias)
            weights = (gram * dec).astype(BF)
            turned.append(dot(dy_t[h * psize : (h + 1) * psize, :], weights))
            mine = (lane >= e * psize) & (lane < (e + 1) * psize)
            left = jnp.where(mine, dy[:, j : j + w], 0.0).astype(BF)
            dgram += dot_nt(left, scaled_b[:, j : j + w]) * dec
    gsc = jnp.concatenate(turned, axis=0).T
    ds_b = ds[...].astype(BF)
    st_b = st_r[0]
    ein_e = expand(tcol, 2 * HP, width, psize)
    eout_e = expand(tcol, 3 * HP, width, psize)
    gsc += eout_e * dot(b_b, ds_b)
    sent = (eout_e * scaled).astype(BF)
    seen = (ein_e * dy).astype(BF)
    dgram_b = dgram.astype(BF)
    gb = dot_tn(dgram_b, c_b) + dot_nt(sent, ds_b)
    gc = dot(dgram_b, b_b) + dot_nt(seen, st_b)
    ds[...] = ein_e[size - 1 : size, :] * ds[...] + dot_tn(c_b, seen)

    y_ns = y - skip * xs
    sums = head_sums(dy_b.astype(F32) * y_ns - scaled_b.astype(F32) * gsc, 0, psize)
    sums += head_sums(gsc * xs, HP, psize) + head_sums(dy * xs, 2 * HP, psize)
    sums = sums.T
    gcum = sums[0:HP, :]
    gdecay = rows_dot(gcum, jnp.where(mask, 1.0, 0.0).astype(BF)) + gcar[:, 0:1] * rows[3:4, :]
    gcar[:, 0:1] = gdecay[:, 0:1]
    gstep = sums[HP : 2 * HP, :] + gdecay * rate
    gdtv = gstep * sigmoid(dtv_r[...])
    gh[:, 0:1] += jnp.sum(gdecay * decay, axis=1, keepdims=True)
    gh[:, 1:2] += jnp.sum(gdtv, axis=1, keepdims=True)
    gh[:, 2:3] += jnp.sum(sums[2 * HP : 3 * HP, :], axis=1, keepdims=True)
    gwdt[...] += dot(gdtv.astype(BF), normed)
    gdt_col = columns_of(gdtv)[:, 0:HP].astype(BF)

    gxp = (dy * skip + gsc * step_e) * (xsig * (1.0 + xpre * (1.0 - xsig)))
    xraw = xraw_r[...]
    bcraw = bcraw_r[...]
    gbp = jnp.concatenate([gb, gc], axis=1) * (bcsig * (1.0 + bcpre * (1.0 - bcsig)))
    xbuf[0:size, :] = gxp
    bcbuf[0:size, :] = gbp
    gx = cx[3:4, :] * gxp
    gbc = cbc[3:4, :] * gbp
    gcx[3:4, :] += jnp.sum(gxp * xraw, axis=0, keepdims=True)
    gcbc[3:4, :] += jnp.sum(gbp * bcraw, axis=0, keepdims=True)
    gcx[4:5, :] += jnp.sum(gxp, axis=0, keepdims=True)
    gcbc[4:5, :] += jnp.sum(gbp, axis=0, keepdims=True)
    for lag in (1, 2, 3):
        keep = tcol[:, 4 * HP + 6 + lag : 4 * HP + 7 + lag]
        moved = xbuf[lag : lag + size, :] * keep
        gx += cx[3 - lag : 4 - lag, :] * moved
        gcx[3 - lag : 4 - lag, :] += jnp.sum(moved * xraw, axis=0, keepdims=True)
        moved = bcbuf[lag : lag + size, :] * keep
        gbc += cbc[3 - lag : 4 - lag, :] * moved
        gcbc[3 - lag : 4 - lag, :] += jnp.sum(moved * bcraw, axis=0, keepdims=True)
    xbuf[size:, :] = gxp[0:TAIL, :]
    bcbuf[size:, :] = gbp[0:TAIL, :]
    gx_b = gx.astype(BF)
    gbc_b = gbc.astype(BF)
    nt = normed.T
    awz[...] += dot(nt, ggate_b)
    awx[...] += dot(nt, gx_b)
    awbc[...] += dot(nt, gbc_b)
    part = dot_nt(ggate_b, wz[...]) + dot_nt(gx_b, wx[...]) + dot_nt(gbc_b, wbc[...]) + dot(gdt_col, wd_s[...].astype(BF))
    part_o[...] = part.astype(BF)
    gnwp[0:1, :] += jnp.sum(part * (inputs * in_rstd), axis=0, keepdims=True)

    if final:

        @pl.when(pid == last)
        def _():
            if width % 128:
                packed_o[...] = jnp.zeros_like(packed_o)
            me = me_r[0]
            pack.put(packed_o, "wz", awz, me)
            pack.put(packed_o, "wx", awx, me)
            if pack.turned:
                turn_s[...] = awo[...].T
                pack.put(packed_o, "wo", turn_s, me)
            else:
                pack.put(packed_o, "wo", awo, me)
            pack.put(packed_o, "wbc", awbc, me)
            heads_t = square([gh[...]]).T[0:HP, :]
            sm_s[...] = square(tiles_of(gwdt[...]) + tiles_of(gcx[...]) + tiles_of(ggn[...]) + [heads_t])
            pack.put(packed_o, "sm", sm_s, me)
            zs_s[...] = square(tiles_of(gcbc[...]) + tiles_of(gnwp[...]))
            pack.put(packed_o, "zs", zs_s, me)


def unpack_kernel(
    pack, heads, me_r, packed, other,
    gnw_o, gwz_o, gwx_o, gwbc_o, gwdt_o, gcx_o, gcxb_o, gcbc_o, gcbcb_o, gdtb_o, gal_o, gds_o, ggn_o, gwo_o,
    sm, zs, turn_s,
):
    me = me_r[0]
    half = pack.shards // 2
    for ref, slots in ((packed, range(half)), (other, range(half, 2 * half))):
        pack.take(ref, "wz", gwz_o, me, slots)
        pack.take(ref, "wx", gwx_o, me, slots)
        pack.take(ref, "wo", turn_s if pack.turned else gwo_o, me, slots)
        pack.take(ref, "wbc", gwbc_o, me, slots)
        pack.take(ref, "sm", sm, me, slots)
        pack.take(ref, "zs", zs, me, slots)
    if pack.turned:
        gwo_o[...] = turn_s[...].T
    dim, width = gwz_o.shape

    def wide(ref, at, total):
        tiles = [ref[at + 8 * t : at + 8 * t + 8, 0:w] for t, (j, w) in enumerate(lane_tiles(total))]
        return jnp.concatenate(tiles, axis=1) if len(tiles) > 1 else tiles[0], at + 8 * len(tiles)

    gwdt, at = wide(sm, 0, dim)
    gcx, at = wide(sm, at, width)
    ggn, at = wide(sm, at, width)
    gh = sm[at : at + 8, :]
    gcbc, at = wide(zs, 0, gcbc_o.shape[1])
    gnw, at = wide(zs, at, dim)
    gwdt_o[...] = gwdt[0:heads]
    gcx_o[...] = gcx[0:4]
    gcxb_o[...] = gcx[4]
    gcbc_o[...] = gcbc[0:4]
    gcbcb_o[...] = gcbc[4]
    gnw_o[...] = gnw[0]
    ggn_o[...] = ggn[0]
    gal_o[...] = gh[0, 0:heads]
    gdtb_o[...] = gh[1, 0:heads]
    gds_o[...] = gh[2, 0:heads]


def block_kernel(di, inner_r, hid, own_r, got_r, stats_r, *rest):
    block_o = rest[-1]
    size = hid.shape[0]
    col = columns_of(lax.rsqrt(stats_r[...] / di + EPS))[:, 0:1]
    mixed = jnp.where(inner_r[0] == 1, own_r[...].astype(F32), got_r[...].astype(F32))
    block_o[...] = (hid[...].astype(F32) + col * mixed).astype(BF)


def ingrad_kernel(inner_r, hid, og, own_r, got_r, nw, *rest):
    ingrad_o = rest[-1]
    inputs = hid[...].astype(F32)
    rstd = lax.rsqrt(jnp.mean(inputs * inputs, axis=1, keepdims=True) + EPS)
    gn = jnp.where(inner_r[0] == 1, own_r[...].astype(F32), got_r[...].astype(F32)) * row_of(nw)
    mean = jnp.mean(gn * inputs, axis=1, keepdims=True)
    ingrad_o[...] = og[...].astype(F32) + rstd * gn - inputs * (rstd * rstd * rstd * mean)


def swap(value, axis, count, mask):
    return lax.ppermute(value, axis, [(i, i ^ mask) for i in range(count)])


def plus(a, b):
    return (a.astype(F32) + b.astype(F32)).astype(a.dtype)


def local(
    hidden_in, segment_ids, norm_weight, w_z, w_x, w_bc, w_dt, conv_x, conv_x_bias, conv_bc, conv_bc_bias,
    dt_bias, a_log, d_skip, gate_norm_weight, w_out, out_grad, n_tensor, n_dp,
):
    total = segment_ids.shape[1]
    dim = hidden_in.shape[1]
    heads = dt_bias.shape[0]
    width = w_z.shape[1]
    psize = width // heads
    nst = w_bc.shape[1] // 2
    di = width * n_tensor
    size = CHUNK
    half = total // 2
    nh = half // size
    wdt = w_dt.T
    me = jnp.reshape(lax.axis_index("dp"), (1,)).astype(jnp.int32)

    def whole(a):
        return pl.BlockSpec(a.shape, lambda i: (0,) * len(a.shape))

    def out(shape, dt):
        return jax.ShapeDtypeStruct(shape, dt)

    def cost(us):
        return pl.CostEstimate(flops=int(us * 1.0e9), bytes_accessed=int(us * 3.0e6), transcendentals=0)

    kept = [(TAIL, width), (TAIL, 2 * nst), (nst, width)]
    params = [pltpu.VMEM((16, total), F32), pltpu.VMEM((HP, dim), F32), pltpu.VMEM((HP, 128), F32)]

    def full(s):
        return pl.BlockSpec(s, lambda i: (0,) * len(s))

    def forward(part, carry):
        c0 = part * nh

        def tok(w):
            return pl.BlockSpec((size, w), lambda i: (i, 0))

        def src(w):
            return pl.BlockSpec((size, w), lambda i: (i + c0, 0))

        def rowf(h):
            return pl.BlockSpec((h, size), lambda i: (0, i))

        fixed = (
            segment_ids, norm_weight, w_z, w_x, w_bc, wdt, conv_x, conv_x_bias, conv_bc, conv_bc_bias, dt_bias,
            a_log, d_skip, gate_norm_weight, w_out,
        ) + carry
        return pl.pallas_call(
            functools.partial(fwd_kernel, psize, c0),
            grid=(nh,),
            in_specs=[src(dim), src(dim)] + [whole(a) for a in fixed],
            out_specs=[
                tok(dim), tok(width), tok(width), tok(width), tok(2 * nst), tok(2 * nst), rowf(HP), tok(width), tok(width),
                pl.BlockSpec((1, nst, width), lambda i: (i, 0, 0)), tok(dim), rowf(HP),
            ] + [full(a) for a in kept],
            out_shape=[
                out((half, dim), BF), out((half, width), F32), out((half, width), F32), out((half, width), F32),
                out((half, 2 * nst), F32), out((half, 2 * nst), F32), out((HP, half), F32), out((half, width), F32),
                out((half, width), F32), out((nh, nst, width), BF), out((half, dim), BF), out((HP, half), F32),
            ] + [out(a, F32) for a in kept],
            scratch_shapes=[
                pltpu.VMEM((size + TAIL, width), F32), pltpu.VMEM((size + TAIL, 2 * nst), F32), pltpu.VMEM((nst, width), F32),
            ] + params,
            cost_estimate=cost(9),
            name="fwd",
        )(hidden_in, out_grad, *fixed)

    pack = Pack(dim, width, 2 * nst, n_dp)
    accs = [
        (dim, width), (dim, width), (dim, 2 * nst), (width, dim), (HP, dim), (HP, width), (HP, 2 * nst), (HP, width), (HP, dim),
        (HP, 128), (size + TAIL, width), (size + TAIL, 2 * nst), (nst, width), (HP, 128),
    ]

    def backward(part, saved, stats, carried):
        c0 = part * nh
        final = carried is not None

        def tok(w):
            return pl.BlockSpec((size, w), lambda i: (nh - 1 - i, 0))

        def src(w):
            return pl.BlockSpec((size, w), lambda i: (c0 + nh - 1 - i, 0))

        def rowb(h):
            return pl.BlockSpec((h, size), lambda i: (0, nh - 1 - i))

        fixed = (w_z, w_x, w_bc, wdt, conv_x, conv_bc, dt_bias, a_log, d_skip, gate_norm_weight)
        held = tuple(carried) if final else ()
        if final:
            shapes = [out((half, dim), BF), out((pack.shards * pack.rows, 128), BF)]
            specs = [tok(dim), full((pack.shards * pack.rows, 128))]
            turn = (dim, width) if pack.turned else (HP, 128)
            scratch = [pltpu.VMEM(s, F32) for s in accs]
            extra = [pltpu.VMEM((128, 128), F32), pltpu.VMEM((128, 128), F32), pltpu.VMEM(turn, F32)]
        else:
            shapes = [out((half, dim), BF)] + [out(s, F32) for s in accs]
            specs = [tok(dim)] + [full(s) for s in accs]
            scratch = []
            extra = []
        return pl.pallas_call(
            functools.partial(bwd_kernel, psize, di, c0, pack if final else None),
            grid=(nh,),
            in_specs=[
                src(dim), src(dim), whole(segment_ids), tok(dim), tok(width), tok(width), tok(width), tok(2 * nst),
                tok(2 * nst), rowb(HP), tok(width), tok(width),
                pl.BlockSpec((1, nst, width), lambda i: (nh - 1 - i, 0, 0)), rowb(HP),
            ] + [whole(a) for a in fixed] + [pl.BlockSpec(memory_space=pltpu.SMEM)] + [whole(a) for a in held],
            out_specs=specs,
            out_shape=shapes,
            scratch_shapes=scratch + params + extra,
            cost_estimate=cost(15),
            name="bwd",
        )(hidden_in, out_grad, segment_ids, *saved, stats, *fixed, me, *held)

    stride = n_tensor // 4
    place = lax.axis_index("tensor") // stride
    inner = (place == 1) | (place == 2)

    def outer(value):
        return lax.ppermute(value, "tensor", [(z * stride + j, (z ^ 1) * stride + j) for z in range(4) for j in range(stride)])

    def middle(value):
        return lax.ppermute(value, "tensor", [(z * stride + j, (3 - z) * stride + j) for z in (1, 2) for j in range(stride)])

    def joined(value):
        mask = 1
        while mask < stride:
            value = plus(value, swap(value, "tensor", n_tensor, mask))
            mask *= 2
        return value

    def summed(value):
        terms = [value] + [swap(value, "tensor", n_tensor, mask) for mask in range(1, n_tensor)]
        while len(terms) > 1:
            terms = [a + b for a, b in zip(terms[::2], terms[1::2])]
        return terms[0]

    def blk(w, c0=0):
        return pl.BlockSpec((size, w), lambda i: (i + c0, 0))

    def written(part, name, kernel, dt, args, specs, held):
        return pl.pallas_call(
            kernel,
            grid=(nh,),
            in_specs=specs + ([pl.BlockSpec(memory_space=pl.ANY)] if part else []),
            out_specs=blk(dim, (1 - part) * nh),
            out_shape=out((total, dim), dt),
            input_output_aliases={len(args): 0} if part else {},
            cost_estimate=cost(0.01),
            name=name,
        )(*args, *held)

    place_id = jnp.reshape(inner, (1,)).astype(jnp.int32)
    scalar = pl.BlockSpec(memory_space=pltpu.SMEM)

    def block(part, own, got, st, *held):
        specs = [scalar, blk(dim, (1 - part) * nh), blk(dim), blk(dim), pl.BlockSpec((HP, size), lambda i: (0, i))]
        args = (place_id, hidden_in, own, got, st)
        return written(part, "block", functools.partial(block_kernel, di), BF, args, specs, held)

    def ingrad(part, own, got, *held):
        here = blk(dim, (1 - part) * nh)
        specs = [scalar, here, here, blk(dim), blk(dim), whole(norm_weight)]
        args = (place_id, hidden_in, out_grad, own, got, norm_weight)
        return written(part, "ingrad", ingrad_kernel, F32, args, specs, held)

    fa = forward(0, ())
    q0 = joined(fa[10])
    r0 = outer(q0)
    fb = forward(1, tuple(fa[12:15]))
    q1 = joined(fb[10])
    stats = summed(jnp.concatenate([fa[11], fb[11]], axis=1))
    stats_a, stats_b = stats[:, :half], stats[:, half:]
    a0 = plus(q0, r0)
    stats_b, a0 = lax.optimization_barrier((stats_b, a0))
    r1 = outer(q1)
    m0 = middle(a0)
    b1 = backward(1, fb[:10], stats_b, None)
    p1 = joined(b1[0])
    t0 = plus(a0, m0)
    a1 = plus(q1, r1)
    stats_a, t0, a1 = lax.optimization_barrier((stats_a, t0, a1))
    r2 = outer(jnp.where(inner, t0, p1))
    m1 = middle(a1)
    p0, packed = backward(0, fa[:10], stats_a, b1[1:])
    p0 = joined(p0)
    packed, p0, r2, m1 = lax.optimization_barrier((packed, p0, r2, m1))
    ap1 = plus(p1, r2)
    t1 = plus(a1, m1)

    send3 = jnp.where(inner, t1, p0)
    buf, send3, ap1 = lax.optimization_barrier((packed, send3, ap1))
    r3 = outer(send3)
    mp1 = middle(ap1)
    rows = buf.shape[0] // 2
    buf = plus(buf[:rows], swap(buf[rows:], "dp", n_dp, 1))
    slots = range(1, n_dp // 2)
    rows = pack.rows
    terms = [buf[:rows]] + [swap(buf[r * rows : (r + 1) * rows], "dp", n_dp, pack.partner(r)) for r in slots]
    buf = sum(term.astype(F32) for term in terms).astype(BF)
    buf, r3, mp1 = lax.optimization_barrier((buf, r3, mp1))
    ap0 = plus(p0, r3)
    tp1 = plus(ap1, mp1)
    zpart = summed(buf[pack.zstart :].astype(F32)).astype(BF)
    buf = jnp.concatenate([buf[: pack.zstart], zpart])
    r4 = outer(tp1)
    mp0 = middle(ap0)
    block_out = block(1, t0, r2, stats_a, block(0, t1, r3, stats_b))
    buf, r4, mp0, block_out = lax.optimization_barrier((buf, r4, mp0, block_out))
    tp0 = plus(ap0, mp0)
    buf, tp0 = lax.optimization_barrier((buf, tp0))
    r5 = outer(tp0)
    buf = jnp.concatenate([buf] + [swap(buf, "dp", n_dp, pack.partner(r)) for r in slots])

    grad1 = ingrad(0, tp1, r4)
    buf, r5, grad1 = lax.optimization_barrier((buf, r5, grad1))
    other = swap(buf, "dp", n_dp, 1)
    in_grad = ingrad(1, tp0, r5, grad1)
    grads = pl.pallas_call(
        functools.partial(unpack_kernel, pack, heads),
        out_shape=[
            out((dim,), F32), out((dim, width), F32), out((dim, width), F32), out((dim, 2 * nst), F32), out((heads, dim), F32),
            out((4, width), F32), out((width,), F32), out((4, 2 * nst), F32), out((2 * nst,), F32), out((heads,), F32),
            out((heads,), F32), out((heads,), F32), out((width,), F32), out((width, dim), F32),
        ],
        in_specs=[pl.BlockSpec(memory_space=pltpu.SMEM)] + [pl.BlockSpec(memory_space=pltpu.VMEM)] * 2,
        scratch_shapes=[
            pltpu.VMEM((128, 128), F32), pltpu.VMEM((128, 128), F32), pltpu.VMEM((dim, width) if pack.turned else (HP, 128), F32),
        ],
        cost_estimate=cost(0.01),
        name="unpack",
    )(me, buf, other)
    return (block_out, in_grad, *grads[:4], grads[4].T, *grads[5:])

def solution(mesh):
    t = P(None, "tensor")
    return jax.shard_map(
        functools.partial(local, n_tensor=mesh.shape["tensor"], n_dp=mesh.shape["dp"]),
        mesh=mesh,
        in_specs=(
            P("dp", None), P("dp", None), P(), t, t, P(), t, t, P("tensor"), P(), P(),
            P("tensor"), P("tensor"), P("tensor"), P("tensor"), P("tensor", None), P("dp", None),
        ),
        out_specs=(
            P("dp", None), P("dp", None), P(), t, t, P(), t, t, P("tensor"), P(), P(),
            P("tensor"), P("tensor"), P("tensor"), P("tensor"), P("tensor", None),
        ),
        check_vma=False,
    )
```
